128 devices in a mesh: len: 32 (over x, y, core), mem: 4 (over z).
Axes of the slice: x: 4, y: 4, z: 4, core: 2. Of those that a mesh axis runs over, the one named last changes fastest.
Arguments:
- phase_left: float32 [32, 1048576], P('mem', 'len'), may hold values from -3.140625 to 3.140625
- phase_right: float32 [32, 1048576], P('mem', 'len'), may hold values from -3.140625 to 3.140625
- roughness: float32 [32], P('mem'), may hold values from 0.1 to 10
- waviness: float32 [32], P('mem'), may hold values from 1.5 to 2.5
- coherence: float32 [32], P('mem'), may hold values from 32 to 512
Outputs:
- profile: float32 [2, 32, 1048576], P(None, 'mem', 'len')
- r_factor: float32 [32, 32], replicated
The draws below stay inside these ranges and needn't reach their ends.
All inputs are finite; a program needn't handle non-finite values.
Results may differ from the reference program's by a relative error of at most 0.0003.
Values sent between devices are 32-bit elements; how exact they have to be, the bound alone decides.
A program may use at most 128 MiB of HBM per device.

```python
import math
import jax
import jax.numpy as jnp
from jax import lax

OUTER = 1024
INNER = 1024
MEMBERS = 32
ANCHOR = 64
POINTS = 1048576


def block_levels(key, shape, split, low, top_value):
    factor_of, own = 1.0, jax.random.fold_in(key, 6)
    for position, blocks in split:
        draws = jnp.exp(jax.random.uniform(jax.random.fold_in(own, position), (blocks,), jnp.float32, low / len(split), top_value / len(split)))
        factor_of = factor_of * jnp.repeat(draws, shape[position] // blocks).reshape([-1 if axis == position else 1 for axis in range(len(shape))])
    return factor_of


def setup_inputs(seed: int = 0) -> dict:
    splits = jax.random.split(jax.random.key(seed), 6)
    return {
        "phase_left": jnp.clip(jax.random.uniform(splits[0], (MEMBERS, POINTS), jnp.float32, -3.140625, 3.140625), -3.140625, 3.140625),
        "phase_right": jnp.clip(jax.random.uniform(splits[1], (MEMBERS, POINTS), jnp.float32, -3.140625, 3.140625), -3.140625, 3.140625),
        "roughness": jnp.clip(jnp.exp(math.log(10.0) - 4.6051702 * jax.random.uniform(splits[2], (MEMBERS,), jnp.float32) ** block_levels(splits[2], (MEMBERS,), ((0, 4),), -0.2, 0.2)), 0.1, 10.0),
        "waviness": jnp.clip(1.5 + 1.0 * jax.random.uniform(splits[3], (MEMBERS,), jnp.float32) ** block_levels(splits[3], (MEMBERS,), ((0, 4),), -0.2, 0.2), 1.5, 2.5),
        "coherence": jnp.clip(jnp.exp(math.log(512.0) - 2.7725887 * jax.random.uniform(splits[4], (MEMBERS,), jnp.float32) ** block_levels(splits[4], (MEMBERS,), ((0, 4),), -0.2, 0.2)), 32.0, 512.0),
    }


def spectra_of(phase_left, phase_right, roughness, waviness, coherence, freq):
    amplitude = jnp.sqrt(2.0 * roughness * (waviness - 1.0) / ANCHOR)[:, None] * ((freq + ANCHOR) / ANCHOR) ** (-0.5 * waviness[:, None])
    freq_ratio = freq / coherence[:, None]
    coherent = 1.0 / (1.0 + freq_ratio * freq_ratio)
    incoherent = freq_ratio * jnp.sqrt(2.0 + freq_ratio * freq_ratio) * coherent
    cos_left = jnp.cos(phase_left)
    sin_left = jnp.sin(phase_left)
    cos_right = jnp.cos(phase_right)
    sin_right = jnp.sin(phase_right)
    real_part = jnp.stack([amplitude * cos_left, amplitude * (coherent * cos_left + incoherent * cos_right)])
    imag_part = jnp.stack([amplitude * sin_left, amplitude * (coherent * sin_left + incoherent * sin_right)])
    return (real_part, imag_part)

def reference(phase_left, phase_right, roughness, waviness, coherence):
    point_count = OUTER * INNER
    freq = jnp.arange(point_count, dtype=jnp.float32)[None, :]
    real_part, imag_part = spectra_of(phase_left, phase_right, roughness, waviness, coherence, freq)
    spectrum = lax.complex(real_part, imag_part)
    profile = jnp.real(jnp.fft.ifft(spectrum, axis=-1)) * point_count
    profile = profile.astype(real_part.dtype)
    snapshot = jnp.transpose(profile, (0, 2, 1)).reshape(2 * point_count, MEMBERS) / jnp.sqrt(jnp.float32(2 * point_count))
    upper = jnp.linalg.qr(snapshot, mode='r')
    r_factor = upper * jnp.sign(jnp.diagonal(upper))[:, None]
    return (profile, r_factor)
```

```python
import functools
import math

import jax
import jax.numpy as jnp
import ml_dtypes
import numpy as np
from jax import lax
from jax.experimental import pallas as pl
from jax.experimental.pallas import tpu as pltpu
from jax.sharding import PartitionSpec as P

ANCHOR = 64
POINTS = 1048576
LEN = 32
MEM = 4
ROWS = 128
LANES = 128
F32 = jnp.float32
BF16 = jnp.bfloat16
MESH = pl.DeviceIdType.MESH
VMEM_LIMIT = 56 * 1024 * 1024


def halves(table):
    table = np.asarray(table, np.float64)
    high = table.astype(np.float32).astype(ml_dtypes.bfloat16)
    low = (table - high.astype(np.float64)).astype(np.float32).astype(ml_dtypes.bfloat16)
    return np.stack([high, low])


def class_of():
    d = np.arange(LEN)
    rest = np.where(d == 0, 64, 128 - d)
    third = np.where(d == 0, 32, 64 - d)
    fourth = np.where(d == 0, 96, 64 + d)
    return np.stack([d, rest, third, fourth], axis=1)


@functools.lru_cache(None)
def tables():
    turn = 2.0 * math.pi
    w_row = np.arange(ROWS)
    w = w_row // 16 + 8 * (w_row % 16)
    r = np.arange(ROWS)
    row_tables = []
    for a in range(4):
        angle = turn * ((w[:, None] * r[None, :] % 128) / 128.0 + a * r[None, :] / 512.0)
        cos, sin = np.cos(angle), np.sin(angle)
        row_tables.append(halves(np.block([[cos, -sin], [sin, cos]])))
    row_dft = np.stack(row_tables)
    lane = np.arange(LANES)
    e, m = lane // 8, lane % 8
    same = (m[:, None] == m[None, :]).astype(np.float64)
    angle = turn * (e[:, None] * e[None, :] % 16) / 16.0
    cos, sin = 0.5 * same * np.cos(angle), 0.5 * same * np.sin(angle)
    lane_dft = halves(np.block([[cos, sin], [-sin, cos]]))
    v = np.arange(128)
    c = class_of().reshape(-1)
    angle = turn * (v[:, None] * c[None, :] % 128) / 128.0
    cos, sin = np.cos(angle), np.sin(angle)
    class_dft = halves(np.block([[cos, -sin], [sin, cos]]))
    upper = np.arange(4)[:, None] + 4 * w[None, :]
    angle = turn * (upper.reshape(-1)[:, None] * e[None, :]) / 8192.0
    twist = np.stack([np.cos(angle), np.sin(angle)]).astype(np.float32)
    fold = np.zeros((512, 32), np.float32)
    index = np.arange(512)
    fold[index, 8 * (index // 128) + index % 8] = 1.0
    return row_dft, lane_dft, class_dft, twist, fold, upper.reshape(-1)


@functools.lru_cache(None)
def sine_terms():
    h = np.cos(np.pi * (np.arange(4000) + 0.5) / 4000) * 1.575
    z = h * h
    sin = np.linalg.lstsq(np.stack([h ** (2 * n + 1) for n in range(6)], 1), np.sin(h), rcond=None)[0]
    cos = np.linalg.lstsq(np.stack([z**n for n in range(1, 7)], 1), np.cos(h) - 1.0, rcond=None)[0]
    return [float(x) for x in sin], [float(x) for x in cos]


def cos_sin(phase):
    sin_terms, cos_terms = sine_terms()
    half = phase * 0.5
    z = half * half
    s = jnp.full_like(z, sin_terms[-1])
    for term in sin_terms[-2::-1]:
        s = s * z + term
    s = s * half
    c = jnp.full_like(z, cos_terms[-1])
    for term in cos_terms[-2::-1]:
        c = c * z + term
    c = c * z + 1.0
    return 1.0 - 2.0 * (s * s), 2.0 * (s * c)


def split(x):
    high = x.astype(BF16)
    return high, (x - high.astype(F32)).astype(BF16)


def dot(a, b):
    return jnp.dot(a, b, preferred_element_type=F32)


def sort_kernel(left_ref, right_ref, out_ref):
    for index, ref in enumerate((left_ref, right_ref)):

        def step(i, carry, index=index, ref=ref):
            tiles = [ref[:, pl.ds(pl.multiple_of(i * 2048 + e * 128, 128), 128)] for e in range(16)]
            block = jnp.concatenate(tiles, axis=0)
            out_ref[pl.ds(index * 16 + i, 128, stride=32), :] = block.T
            return carry

        lax.fori_loop(0, 16, step, 0)


def sort_phases(left, right):
    return pl.pallas_call(
        sort_kernel,
        out_shape=jax.ShapeDtypeStruct((4096, LANES), F32),
        compiler_params=pltpu.CompilerParams(vmem_limit_bytes=VMEM_LIMIT),
        name="sort_phases",
    )(left, right)


def meet(partners):
    barrier = pltpu.get_barrier_semaphore()
    total = 0
    for axis, size in partners:
        me = lax.axis_index(axis)

        def greet(r, carry, axis=axis, size=size, me=me):
            pl.semaphore_signal(barrier, inc=1, device_id={axis: lax.rem(me + r, size)}, device_id_type=MESH)
            return carry

        lax.fori_loop(1, size, greet, 0)
        total += size - 1
    pl.semaphore_wait(barrier, total)


def exchange1_kernel(src, dst, send, recv, own):
    me = lax.axis_index("len")
    meet([("len", LEN)])

    def classes(d):
        first = d == 0
        return (d, jnp.where(first, 64, 128 - d), jnp.where(first, 32, 64 - d), jnp.where(first, 96, 64 + d))

    mine = [pltpu.make_async_copy(src.at[c], dst.at[me, slot], own.at[slot]) for slot, c in enumerate(classes(me))]
    for copy in mine:
        copy.start()

    def start(r, carry):
        d = lax.rem(me + r, LEN)
        for slot, c in enumerate(classes(d)):
            pltpu.make_async_remote_copy(
                src.at[c], dst.at[me, slot], send.at[r], recv.at[r], device_id={"len": d}, device_id_type=MESH
            ).start()
        return carry

    lax.fori_loop(1, LEN, start, 0)
    for copy in mine:
        copy.wait()

    def finish(r, carry):
        source = lax.rem(me + LEN - r, LEN)
        whole = pltpu.make_async_remote_copy(
            dst.at[source], dst.at[source], send.at[r], recv.at[r], device_id={"len": source}, device_id_type=MESH
        )
        whole.wait_send()
        whole.wait_recv()
        return carry

    lax.fori_loop(1, LEN, finish, 0)


def exchange1(sorted_phases):
    return pl.pallas_call(
        exchange1_kernel,
        out_shape=jax.ShapeDtypeStruct((LEN, 4, 32, LANES), F32),
        in_specs=[pl.BlockSpec(memory_space=pl.ANY)],
        out_specs=pl.BlockSpec(memory_space=pl.ANY),
        scratch_shapes=[
            pltpu.SemaphoreType.DMA((LEN,)),
            pltpu.SemaphoreType.DMA((LEN,)),
            pltpu.SemaphoreType.DMA((4,)),
        ],
        compiler_params=pltpu.CompilerParams(collective_id=0, has_side_effects=True),
        name="exchange_phases",
    )(sorted_phases)


def exchange_kernel(with_mem, src, *refs):
    if with_mem:
        dst, dst_mem, send, recv, own, send_mem, recv_mem, own_mem = refs
    else:
        dst, send, recv, own = refs
    me = lax.axis_index("len")
    meet([("len", LEN), ("mem", MEM)] if with_mem else [("len", LEN)])
    mine = [pltpu.make_async_copy(src.at[me], dst.at[me], own)]
    if with_mem:
        my_mem = lax.axis_index("mem")
        quarter = LEN // MEM
        mine.append(pltpu.make_async_copy(src.at[pl.ds(my_mem * quarter, quarter)], dst_mem.at[my_mem], own_mem))
    for copy in mine:
        copy.start()

    def start(r, carry):
        d = lax.rem(me + r, LEN)
        pltpu.make_async_remote_copy(
            src.at[d], dst.at[me], send.at[r], recv.at[r], device_id={"len": d}, device_id_type=MESH
        ).start()
        return carry

    lax.fori_loop(1, LEN, start, 0)
    if with_mem:

        def start_mem(r, carry):
            d = lax.rem(my_mem + r, MEM)
            pltpu.make_async_remote_copy(
                src.at[pl.ds(d * quarter, quarter)],
                dst_mem.at[my_mem],
                send_mem.at[r],
                recv_mem.at[r],
                device_id={"mem": d},
                device_id_type=MESH,
            ).start()
            return carry

        lax.fori_loop(1, MEM, start_mem, 0)
    for copy in mine:
        copy.wait()

    def finish(r, carry):
        source = lax.rem(me + LEN - r, LEN)
        whole = pltpu.make_async_remote_copy(
            dst.at[source], dst.at[source], send.at[r], recv.at[r], device_id={"len": source}, device_id_type=MESH
        )
        whole.wait_send()
        whole.wait_recv()
        return carry

    lax.fori_loop(1, LEN, finish, 0)
    if with_mem:

        def finish_mem(r, carry):
            source = lax.rem(my_mem + MEM - r, MEM)
            whole = pltpu.make_async_remote_copy(
                dst_mem.at[source],
                dst_mem.at[source],
                send_mem.at[r],
                recv_mem.at[r],
                device_id={"mem": source},
                device_id_type=MESH,
            )
            whole.wait_send()
            whole.wait_recv()
            return carry

        lax.fori_loop(1, MEM, finish_mem, 0)


def exchange(blocks, collective, with_mem):
    blocks = blocks.reshape(LEN, ROWS, LANES)
    out_shape = [jax.ShapeDtypeStruct((LEN, ROWS, LANES), F32)]
    scratch = [pltpu.SemaphoreType.DMA((LEN,)), pltpu.SemaphoreType.DMA((LEN,)), pltpu.SemaphoreType.DMA]
    if with_mem:
        out_shape.append(jax.ShapeDtypeStruct((MEM, LEN // MEM, ROWS, LANES), F32))
        scratch += [pltpu.SemaphoreType.DMA((MEM,)), pltpu.SemaphoreType.DMA((MEM,)), pltpu.SemaphoreType.DMA]
    return pl.pallas_call(
        functools.partial(exchange_kernel, with_mem),
        out_shape=out_shape,
        in_specs=[pl.BlockSpec(memory_space=pl.ANY)],
        out_specs=[pl.BlockSpec(memory_space=pl.ANY)] * len(out_shape),
        scratch_shapes=scratch,
        compiler_params=pltpu.CompilerParams(collective_id=collective, has_side_effects=True),
        name="exchange_%d" % collective,
    )(blocks)


def partial_kernel(
    slots_ref, phases_ref, member_ref, column_ref, turn_ref, row_ref, lane_ref, twist_ref, out_ref, high_ref, low_ref, part_ref
):
    level = member_ref[0:1, :]
    exponent = member_ref[1:2, :]
    inverse = member_ref[2:3, :]

    def spectra(index, carry):
        slot = lax.div(index, 8)
        low_p = lax.rem(index, 8)
        row = lax.broadcasted_iota(jnp.int32, (16, LANES), 0)
        lane = lax.broadcasted_iota(jnp.int32, (16, LANES), 1)
        offset = row * 2048 + lax.div(lane, 8) * 128 + slots_ref[slot]
        parts = []
        for q in range(4):
            p = 8 * q + low_p
            freq = (offset + p * 32768).astype(F32)
            amplitude = level * jnp.exp(exponent * jnp.log(freq * (1.0 / ANCHOR) + 1.0))
            ratio = freq * inverse
            square = ratio * ratio
            coherent = 1.0 / (1.0 + square)
            incoherent = ratio * jnp.sqrt(2.0 + square) * coherent
            cos_left, sin_left = cos_sin(phases_ref[p, slot, 0:16, :])
            cos_right, sin_right = cos_sin(phases_ref[p, slot, 16:32, :])
            first, second = amplitude * coherent, amplitude * incoherent
            parts.append(
                (
                    amplitude * cos_left,
                    amplitude * sin_left,
                    first * cos_left + second * cos_right,
                    first * sin_left + second * sin_right,
                )
            )
        rows = pl.ds(pl.multiple_of(low_p * 16, 16), 16)
        imag_rows = pl.ds(pl.multiple_of(128 + low_p * 16, 16), 16)
        for track in range(2):
            re = [part[2 * track] for part in parts]
            im = [part[2 * track + 1] for part in parts]
            even_re, even_im = re[0] + re[2], im[0] + im[2]
            odd_re, odd_im = re[1] + re[3], im[1] + im[3]
            diff_re, diff_im = re[0] - re[2], im[0] - im[2]
            skew_re, skew_im = re[1] - re[3], im[1] - im[3]
            results = (
                (even_re + odd_re, even_im + odd_im),
                (diff_re - skew_im, diff_im + skew_re),
                (even_re - odd_re, even_im - odd_im),
                (diff_re + skew_im, diff_im - skew_re),
            )
            lanes = slice(track * 128, track * 128 + 128)
            for a, (x, y) in enumerate(results):
                high, low = split(x)
                high_ref[a, slot, rows, lanes] = high
                low_ref[a, slot, rows, lanes] = low
                high, low = split(y)
                high_ref[a, slot, imag_rows, lanes] = high
                low_ref[a, slot, imag_rows, lanes] = low
        return carry

    lax.fori_loop(0, 32, spectra, 0)
    is_first = slots_ref[0] == 0

    def transform(a, carry):
        table_high, table_low = row_ref[a, 0], row_ref[a, 1]
        twist_cos, twist_sin = twist_ref[0, a], twist_ref[1, a]
        for slot in range(4):
            high, low = high_ref[a, slot], low_ref[a, slot]
            partial = dot(table_high, high) + dot(table_low, high) + dot(table_high, low)
            column_cos = column_ref[a, :, 2 * slot : 2 * slot + 1]
            column_sin = column_ref[a, :, 2 * slot + 1 : 2 * slot + 2]
            cos = twist_cos * column_cos - twist_sin * column_sin
            sin = twist_cos * column_sin + twist_sin * column_cos
            stacked = []
            for track in range(2):
                re = partial[:128, track * 128 : track * 128 + 128]
                im = partial[128:, track * 128 : track * 128 + 128]
                stacked.append(jnp.concatenate([re * cos - im * sin, re * sin + im * cos], axis=1))
            high, low = split(jnp.concatenate(stacked, axis=0))
            done = dot(high, lane_ref[0]) + dot(low, lane_ref[0]) + dot(high, lane_ref[1])
            cos, sin = turn_ref[2 * slot : 2 * slot + 1, :], turn_ref[2 * slot + 1 : 2 * slot + 2, :]
            re, im = done[:, :128], done[:, 128:]
            part_ref[slot, 0] = re * cos - im * sin
            part_ref[slot, 1] = re * sin + im * cos
        for slot in (0, 2):
            re0, im0 = part_ref[slot, 0, :128, :], part_ref[slot, 1, :128, :]
            re1, im1 = part_ref[slot, 0, 128:, :], part_ref[slot, 1, 128:, :]
            mirror_re0, mirror_im0 = part_ref[slot + 1, 0, :128, :], part_ref[slot + 1, 1, :128, :]
            mirror_re1, mirror_im1 = part_ref[slot + 1, 0, 128:, :], part_ref[slot + 1, 1, 128:, :]
            sum_re0, sum_re1 = re0 + mirror_re0, re1 + mirror_re1
            gap_im0, gap_im1 = im0 - mirror_im0, im1 - mirror_im1
            pair = [
                [sum_re0 - gap_im1, gap_im0 + sum_re1],
                [sum_re0 + gap_im1, sum_re1 - gap_im0],
            ]
            if slot == 0:
                alone = [[re0 + re0, re1 + re1], [mirror_re0 + mirror_re0, mirror_re1 + mirror_re1]]
                pair = [[jnp.where(is_first, alone[n][x], pair[n][x]) for x in range(2)] for n in range(2)]
            for n in range(2):
                for x in range(2):
                    out_ref[:, a, slot + n, x] = pair[n][x].reshape(8, 16, LANES)
        return carry

    lax.fori_loop(0, 4, transform, 0)


def partial_transforms(slots, phases, member_rows, columns, turns):
    row_dft, lane_dft, _, twist, _, _ = tables()
    smem = pl.BlockSpec(memory_space=pltpu.SMEM)
    vmem = pl.BlockSpec(memory_space=pltpu.VMEM)
    return pl.pallas_call(
        partial_kernel,
        out_shape=jax.ShapeDtypeStruct((8, 4, 4, 2, 16, LANES), F32),
        in_specs=[smem] + [vmem] * 7,
        out_specs=vmem,
        scratch_shapes=[
            pltpu.VMEM((4, 4, 256, 256), BF16),
            pltpu.VMEM((4, 4, 256, 256), BF16),
            pltpu.VMEM((4, 2, 256, LANES), F32),
        ],
        compiler_params=pltpu.CompilerParams(vmem_limit_bytes=VMEM_LIMIT),
        name="partial_transforms",
    )(
        slots,
        phases,
        member_rows,
        columns,
        turns,
        jnp.asarray(row_dft),
        jnp.asarray(lane_dft),
        jnp.asarray(twist.reshape(2, 4, ROWS, LANES)),
    )


def gram_kernel(blocks_ref, fold_ref, out_ref, total_ref):
    total_ref[...] = jnp.zeros_like(total_ref)
    contract = (((0,), (0,)), ((), ()))

    def step(n, carry):
        rows = [blocks_ref[z, pl.ds(pl.multiple_of(n * 256, 256), 256), :] for z in range(MEM)]
        high, low = split(jnp.concatenate(rows, axis=1))
        product = functools.partial(lax.dot_general, dimension_numbers=contract, preferred_element_type=F32)
        total_ref[...] += product(high, high) + product(low, high) + product(high, low)
        return carry

    lax.fori_loop(0, 4, step, 0)
    row = lax.broadcasted_iota(jnp.int32, (512, 512), 0)
    column = lax.broadcasted_iota(jnp.int32, (512, 512), 1)
    same = lax.rem(lax.div(row, 8), 16) == lax.rem(lax.div(column, 8), 16)
    kept = jnp.where(same, total_ref[...], 0.0)
    exact = functools.partial(jnp.dot, preferred_element_type=F32, precision=lax.Precision.HIGHEST)
    right = exact(kept, fold_ref[...])
    out_ref[...] = exact(fold_ref[...].T, right) * (128.0 / (2.0 * POINTS))


def gram_part(blocks):
    return pl.pallas_call(
        gram_kernel,
        out_shape=jax.ShapeDtypeStruct((32, 32), F32),
        scratch_shapes=[pltpu.VMEM((512, 512), F32)],
        compiler_params=pltpu.CompilerParams(vmem_limit_bytes=VMEM_LIMIT),
        name="gram_part",
    )(blocks.reshape(MEM, 1024, LANES), jnp.asarray(tables()[4]))


def class_kernel(blocks_ref, table_ref, out_ref):
    def step(n, carry):
        columns = []
        for u2 in (2 * n, 2 * n + 1):
            re = blocks_ref[pl.ds(u2, 128, stride=32), :]
            im = blocks_ref[pl.ds(16 + u2, 128, stride=32), :]
            columns.append(jnp.concatenate([re, im], axis=0))
        high, low = split(jnp.concatenate(columns, axis=1))
        done = dot(table_ref[0], high) + dot(table_ref[1], high) + dot(table_ref[0], low)
        for index in range(2):
            for track in range(2):
                out_ref[pl.ds(16 * track + 2 * n + index, 128, stride=32), :] = done[
                    track * 128 : track * 128 + 128, index * 128 : index * 128 + 128
                ]
        return carry

    lax.fori_loop(0, 8, step, 0)


def class_transform(blocks):
    return pl.pallas_call(
        class_kernel,
        out_shape=jax.ShapeDtypeStruct((4096, LANES), F32),
        compiler_params=pltpu.CompilerParams(vmem_limit_bytes=VMEM_LIMIT),
        name="class_transform",
    )(blocks.reshape(4096, LANES), jnp.asarray(tables()[2]))


def place_kernel(blocks_ref, out_ref):
    def step(index, carry):
        vl = lax.div(index, 8)
        track = lax.rem(lax.div(index, 4), 2)
        high_u2 = lax.rem(index, 4)
        base = vl * 32 + track * 16 + high_u2 * 4
        rows = [blocks_ref[pl.ds(base + low, 32, stride=128), :] for low in range(4)]
        turned = jnp.concatenate(rows, axis=0).T
        for u3 in range(16):
            column = pl.multiple_of((vl * 64 + u3 * 4 + high_u2) * 128, 128)
            out_ref[track, :, pl.ds(column, 128)] = turned[8 * u3 : 8 * u3 + 8, :]
        return carry

    lax.fori_loop(0, 32, step, 0)


def place(blocks):
    return pl.pallas_call(
        place_kernel,
        out_shape=jax.ShapeDtypeStruct((2, 8, 32768), F32),
        compiler_params=pltpu.CompilerParams(vmem_limit_bytes=VMEM_LIMIT),
        name="place_profile",
    )(blocks.reshape(4096, LANES))


def device_tables(me):
    upper = tables()[5]
    first = me == 0
    slots = jnp.stack(
        [me, jnp.where(first, 64, 128 - me), jnp.where(first, 32, 64 - me), jnp.where(first, 96, 64 + me)]
    ).astype(jnp.int32)
    turn = 2.0 * math.pi
    angle = (jnp.asarray(upper, jnp.int32)[:, None] * slots[None, :]).astype(F32) * (turn / POINTS)
    columns = jnp.stack([jnp.cos(angle), jnp.sin(angle)], axis=2).reshape(4, ROWS, 8)
    angle = (jnp.asarray(np.arange(LANES) // 8, jnp.int32)[None, :] * slots[:, None]).astype(F32) * (turn / 2048)
    turns = jnp.stack([jnp.cos(angle), jnp.sin(angle)], axis=1).reshape(8, LANES)
    return slots, columns, turns


def per_device(phase_left, phase_right, roughness, waviness, coherence):
    me = lax.axis_index("len")
    slots, columns, turns = device_tables(me)
    level = jnp.sqrt(2.0 * roughness * (waviness - 1.0) / ANCHOR)
    member_rows = jnp.tile(jnp.stack([level, -0.5 * waviness, 1.0 / coherence]), (1, 16))
    sorted_phases = sort_phases(phase_left, phase_right)
    phases = exchange1(sorted_phases.reshape(128, 32, LANES))
    partial = partial_transforms(slots, phases, member_rows, columns, turns)
    blocks, members = exchange(partial, 1, True)
    gram = lax.psum(gram_part(members), ("len", "mem"))
    outgoing = class_transform(blocks)
    (arrived,) = exchange(outgoing, 2, False)
    profile = place(arrived)
    r_factor = jnp.linalg.cholesky(gram).T
    return profile, r_factor


def solution(mesh):
    placed = (P("mem", "len"), P("mem", "len"), P("mem"), P("mem"), P("mem"))
    return jax.shard_map(
        per_device,
        mesh=mesh,
        in_specs=placed,
        out_specs=(P(None, "mem", "len"), P()),
        check_vma=False,
    )
```

```python
import functools
import math

import jax
import jax.numpy as jnp
import ml_dtypes
import numpy as np
from jax import lax
from jax.experimental import pallas as pl
from jax.experimental.pallas import tpu as pltpu
from jax.sharding import PartitionSpec as P

ANCHOR = 64
POINTS = 1048576
LEN = 32
MEM = 4
ROWS = 128
LANES = 128
F32 = jnp.float32
BF16 = jnp.bfloat16
MESH = pl.DeviceIdType.MESH
VMEM_LIMIT = 56 * 1024 * 1024


def halves(table):
    table = np.asarray(table, np.float64)
    high = table.astype(np.float32).astype(ml_dtypes.bfloat16)
    low = (table - high.astype(np.float64)).astype(np.float32).astype(ml_dtypes.bfloat16)
    return np.stack([high, low])


def class_of():
    d = np.arange(LEN)
    rest = np.where(d == 0, 64, 128 - d)
    third = np.where(d == 0, 32, 64 - d)
    fourth = np.where(d == 0, 96, 64 + d)
    return np.stack([d, rest, third, fourth], axis=1)


@functools.lru_cache(None)
def tables():
    turn = 2.0 * math.pi
    w_row = np.arange(ROWS)
    w = w_row // 16 + 8 * (w_row % 16)
    r = np.arange(ROWS)
    row_tables = []
    for a in range(4):
        angle = turn * ((w[:, None] * r[None, :] % 128) / 128.0 + a * r[None, :] / 512.0)
        cos, sin = np.cos(angle), np.sin(angle)
        row_tables.append(halves(np.block([[cos, -sin], [sin, cos]])))
    row_dft = np.stack(row_tables)
    lane = np.arange(LANES)
    e, m = lane // 8, lane % 8
    same = (m[:, None] == m[None, :]).astype(np.float64)
    angle = turn * (e[:, None] * e[None, :] % 16) / 16.0
    cos, sin = 0.5 * same * np.cos(angle), 0.5 * same * np.sin(angle)
    lane_dft = halves(np.block([[cos, sin], [-sin, cos]]))
    v = np.arange(128)
    c = class_of().reshape(-1)
    angle = turn * (v[:, None] * c[None, :] % 128) / 128.0
    cos, sin = np.cos(angle), np.sin(angle)
    class_dft = halves(np.block([[cos, -sin], [sin, cos]]))
    index = np.arange(512)
    fold = np.zeros((512, LANES), np.float32)
    for a in range(4):
        fold[index, 32 * a + 8 * (index // 128) + index % 8] = 1.0
    return row_dft, lane_dft, class_dft, fold


@functools.lru_cache(None)
def sine_terms():
    h = np.cos(np.pi * (np.arange(4000) + 0.5) / 4000) * 1.575
    z = h * h
    sin = np.linalg.lstsq(np.stack([h ** (2 * n + 1) for n in range(6)], 1), np.sin(h), rcond=None)[0]
    cos = np.linalg.lstsq(np.stack([z**n for n in range(1, 7)], 1), np.cos(h) - 1.0, rcond=None)[0]
    return [float(x) for x in sin], [float(x) for x in cos]


def cos_sin(phase):
    sin_terms, cos_terms = sine_terms()
    half = phase * 0.5
    z = half * half
    s = jnp.full_like(z, sin_terms[-1])
    for term in sin_terms[-2::-1]:
        s = s * z + term
    s = s * half
    c = jnp.full_like(z, cos_terms[-1])
    for term in cos_terms[-2::-1]:
        c = c * z + term
    c = c * z + 1.0
    return 1.0 - 2.0 * (s * s), 2.0 * (s * c)


def split(x):
    high = x.astype(BF16)
    return high, (x - high.astype(F32)).astype(BF16)


def dot(a, b):
    return jnp.dot(a, b, preferred_element_type=F32)


def order():
    ring = lambda n: min(n, 4 - n)
    steps = [(dx, dy, dc) for dc in range(2) for dx in range(4) for dy in range(4) if (dx, dy, dc) != (0, 0, 0)]
    return sorted(steps, key=lambda s: (-ring(s[0]) - ring(s[1]), s[2]))


def partners(me):
    x, y, core = lax.div(me, 8), lax.rem(lax.div(me, 2), 4), lax.rem(me, 2)
    for dx, dy, dc in order():
        yield lax.rem(x + dx, 4) * 8 + lax.rem(y + dy, 4) * 2 + lax.rem(core + dc, 2)


def classes(d):
    first = d == 0
    return (d, jnp.where(first, 64, 128 - d), jnp.where(first, 32, 64 - d), jnp.where(first, 96, 64 + d))


def rows_at(start, size):
    return pl.ds(pl.multiple_of(start, 8), size)


def send(source, target, sems, index, device):
    pltpu.make_async_remote_copy(
        source, target, sems.at[0, index], sems.at[1, index], device_id=device, device_id_type=MESH
    ).start()


def settle(ref, sems, index, device, which):
    copy = pltpu.make_async_remote_copy(
        ref, ref, sems.at[0, index], sems.at[1, index], device_id=device, device_id_type=MESH
    )
    if which == 0:
        copy.wait_send()
    else:
        copy.wait_recv()


def unit_turn(numerator, size):
    cos, sin = cos_sin(numerator.astype(F32) * (2.0 * math.pi / size) - math.pi)
    return -cos, -sin


def sort_phases(index, ref, sorted_ref):
    def step(i, carry):
        tiles = [ref[:, pl.ds(pl.multiple_of(i * 2048 + e * 128, 128), 128)] for e in range(16)]
        sorted_ref[pl.ds(index * 16 + i, 128, stride=32), :] = jnp.concatenate(tiles, axis=0).T
        return carry

    lax.fori_loop(0, 16, step, 0)


def member_lanes(ref):
    lane = lax.rem(lax.broadcasted_iota(jnp.int32, (8, LANES), 1), 8)
    values = jnp.zeros((8, LANES), F32)
    for m in range(8):
        values = jnp.where(lane == m, ref[m], values)
    return values


def fill_levels(pair, me, roughness_ref, waviness_ref, coherence_ref, level_ref):
    waviness = member_lanes(waviness_ref)
    scale = jnp.sqrt(2.0 * member_lanes(roughness_ref) * (waviness - 1.0) * (1.0 / ANCHOR))
    exponent = -0.5 * waviness
    inverse = 1.0 / member_lanes(coherence_ref)
    row = lax.broadcasted_iota(jnp.int32, (8, LANES), 0)
    lane = lax.broadcasted_iota(jnp.int32, (8, LANES), 1)
    spread = row * 2048 + lax.div(lane, 8) * 128
    for half in range(2):
        offset = spread + classes(me)[2 * pair + half]

        def step(n, carry, half=half, offset=offset):
            freq = (offset + n * 16384).astype(F32)
            amplitude = scale * jnp.exp(exponent * jnp.log(freq * (1.0 / ANCHOR) + 1.0))
            ratio = freq * inverse
            square = ratio * ratio
            coherent = 1.0 / (1.0 + square)
            incoherent = ratio * jnp.sqrt(2.0 + square) * coherent
            rows = rows_at(pair * 1024 + half * 512 + n * 8, 8)
            level_ref[0, rows, :] = amplitude
            level_ref[1, rows, :] = amplitude * coherent
            level_ref[2, rows, :] = amplitude * incoherent
            return carry

        lax.fori_loop(0, 64, step, 0, unroll=4)


def fill_twist(pair, me, twist_ref):
    row = lax.broadcasted_iota(jnp.int32, (8, LANES), 0)
    lane = lax.broadcasted_iota(jnp.int32, (8, LANES), 1)
    for half in range(2):
        place = lax.div(lane, 8) * 128 + classes(me)[2 * pair + half]

        def step(n, carry, half=half, place=place):
            upper = lax.div(n, 16) + 4 * lax.rem(lax.div(n, 2), 8) + 32 * (lax.rem(n, 2) * 8 + row)
            cos, sin = unit_turn(lax.rem(upper * place, POINTS), POINTS)
            rows = rows_at(pair * 1024 + half * 512 + n * 8, 8)
            twist_ref[0, rows, :] = cos
            twist_ref[1, rows, :] = sin
            return carry

        lax.fori_loop(0, 64, step, 0, unroll=4)


def spectra(pair, in_ref, level_ref, high_ref, low_ref):
    def step(index, carry):
        half = lax.div(index, 8)
        low_p = lax.rem(index, 8)
        parts = []
        for q in range(4):
            p = 8 * q + low_p
            start = pair * 2048 + p * 64 + half * 32
            cos_left, sin_left = cos_sin(in_ref[rows_at(start, 16), :])
            cos_right, sin_right = cos_sin(in_ref[rows_at(start + 16, 16), :])
            rows = rows_at(pair * 1024 + half * 512 + p * 16, 16)
            amplitude, first, second = level_ref[0, rows, :], level_ref[1, rows, :], level_ref[2, rows, :]
            parts.append(
                (
                    amplitude * cos_left,
                    amplitude * sin_left,
                    first * cos_left + second * cos_right,
                    first * sin_left + second * sin_right,
                )
            )
        rows = pl.ds(pl.multiple_of(low_p * 16, 16), 16)
        imag_rows = pl.ds(pl.multiple_of(128 + low_p * 16, 16), 16)
        for track in range(2):
            re = [part[2 * track] for part in parts]
            im = [part[2 * track + 1] for part in parts]
            even_re, even_im = re[0] + re[2], im[0] + im[2]
            odd_re, odd_im = re[1] + re[3], im[1] + im[3]
            diff_re, diff_im = re[0] - re[2], im[0] - im[2]
            skew_re, skew_im = re[1] - re[3], im[1] - im[3]
            results = (
                (even_re + odd_re, even_im + odd_im),
                (diff_re - skew_im, diff_im + skew_re),
                (even_re - odd_re, even_im - odd_im),
                (diff_re + skew_im, diff_im - skew_re),
            )
            lanes = slice(track * 128, track * 128 + 128)
            for a, (x, y) in enumerate(results):
                high, low = split(x)
                high_ref[a, half, rows, lanes] = high
                low_ref[a, half, rows, lanes] = low
                high, low = split(y)
                high_ref[a, half, imag_rows, lanes] = high
                low_ref[a, half, imag_rows, lanes] = low
        return carry

    lax.fori_loop(0, 16, step, 0)


def transforms(pair, me, high_ref, low_ref, row_ref, lane_ref, twist_ref, part_ref, out_ref):
    is_first = me == 0
    lane = lax.div(lax.broadcasted_iota(jnp.int32, (1, LANES), 1), 8)
    turns = [unit_turn(lane * classes(me)[2 * pair + half], 2048) for half in range(2)]

    def step(a, carry):
        table_high, table_low = row_ref[a, 0], row_ref[a, 1]
        for half in range(2):
            high, low = high_ref[a, half], low_ref[a, half]
            partial = dot(table_high, high) + dot(table_low, high) + dot(table_high, low)
            rows = pl.ds(pl.multiple_of(pair * 1024 + half * 512 + a * 128, 128), 128)
            cos, sin = twist_ref[0, rows, :], twist_ref[1, rows, :]
            stacked = []
            for track in range(2):
                re = partial[:128, track * 128 : track * 128 + 128]
                im = partial[128:, track * 128 : track * 128 + 128]
                stacked.append(jnp.concatenate([re * cos - im * sin, re * sin + im * cos], axis=1))
            high, low = split(jnp.concatenate(stacked, axis=0))
            done = dot(high, lane_ref[0]) + dot(low, lane_ref[0]) + dot(high, lane_ref[1])
            cos, sin = turns[half]
            re, im = done[:, :128], done[:, 128:]
            part_ref[half, 0] = re * cos - im * sin
            part_ref[half, 1] = re * sin + im * cos
        re0, im0 = part_ref[0, 0, :128, :], part_ref[0, 1, :128, :]
        re1, im1 = part_ref[0, 0, 128:, :], part_ref[0, 1, 128:, :]
        mirror_re0, mirror_im0 = part_ref[1, 0, :128, :], part_ref[1, 1, :128, :]
        mirror_re1, mirror_im1 = part_ref[1, 0, 128:, :], part_ref[1, 1, 128:, :]
        sum_re0, sum_re1 = re0 + mirror_re0, re1 + mirror_re1
        gap_im0, gap_im1 = im0 - mirror_im0, im1 - mirror_im1
        packed = [
            [sum_re0 - gap_im1, gap_im0 + sum_re1],
            [sum_re0 + gap_im1, sum_re1 - gap_im0],
        ]
        if pair == 0:
            alone = [[re0 + re0, re1 + re1], [mirror_re0 + mirror_re0, mirror_re1 + mirror_re1]]
            packed = [[jnp.where(is_first, alone[n][x], packed[n][x]) for x in range(2)] for n in range(2)]
        for n in range(2):
            for x in range(2):
                start = (2 * pair + n) * 32 + x * 16
                for wl in range(8):
                    out_ref[4 * wl + a, start : start + 16, :] = packed[n][x][wl * 16 : wl * 16 + 16, :]
        return carry

    lax.fori_loop(0, 4, step, 0)


def gram_part(members_ref, fold_ref, total_ref):
    total_ref[...] = jnp.zeros_like(total_ref)
    product = functools.partial(
        lax.dot_general, dimension_numbers=(((0,), (0,)), ((), ())), preferred_element_type=F32
    )

    def step(n, carry):
        rows = [members_ref[z, pl.ds(2 * n, 2)].reshape(256, LANES) for z in range(MEM)]
        high, low = split(jnp.concatenate(rows, axis=1))
        total_ref[...] += product(high, high) + product(low, high) + product(high, low)
        return carry

    lax.fori_loop(0, 4, step, 0)
    row = lax.broadcasted_iota(jnp.int32, (512, 512), 0)
    column = lax.broadcasted_iota(jnp.int32, (512, 512), 1)
    same = lax.rem(lax.div(row, 8), 16) == lax.rem(lax.div(column, 8), 16)
    kept = jnp.where(same, total_ref[...], 0.0)
    right = jnp.dot(kept, fold_ref[...], preferred_element_type=F32, precision=lax.Precision.HIGHEST)
    row = lax.broadcasted_iota(jnp.int32, (512, LANES), 0)
    lane = lax.broadcasted_iota(jnp.int32, (512, LANES), 1)
    right = jnp.where(lax.div(row, 128) == lax.div(lane, 32), right, 0.0)
    return jnp.sum(right.reshape(64, 8, LANES), axis=0) * (128.0 / (2.0 * POINTS))


def upper_factor(gram):
    row = lax.broadcasted_iota(jnp.int32, (32, LANES), 0)
    lane = lax.broadcasted_iota(jnp.int32, (32, LANES), 1)
    tall = jnp.concatenate([gram] * 4, axis=0)
    tall = jnp.where(lax.div(row, 8) == lax.div(lane, 32), tall, 0.0)
    pick_row = lax.broadcasted_iota(jnp.int32, (LANES, LANES), 0)
    pick_lane = lax.broadcasted_iota(jnp.int32, (LANES, LANES), 1)
    pick = jnp.where(lax.rem(pick_row, 32) == pick_lane, 1.0, 0.0)
    matrix = jnp.dot(tall, pick, preferred_element_type=F32, precision=lax.Precision.HIGHEST)

    def step(n, carry):
        rest, upper = carry
        line = jnp.sum(jnp.where(row == n, rest, 0.0), axis=0, keepdims=True)
        column = jnp.sum(jnp.where(lane == n, rest, 0.0), axis=1, keepdims=True)
        pivot = jnp.sum(jnp.where(lane[0:1] == n, line, 0.0), axis=1, keepdims=True)
        line = jnp.where(lane[0:1] >= n, line / jnp.sqrt(pivot), 0.0)
        column = column / jnp.sqrt(pivot)
        return rest - column * line, jnp.where(row == n, line, upper)

    return lax.fori_loop(0, 32, step, (matrix, jnp.zeros_like(matrix)))[1]


def class_transform(group, in_ref, table_ref, out_ref):
    def step(n, carry):
        columns = []
        for index in range(2):
            u2 = group * 8 + 2 * n + index
            re = in_ref[pl.ds(u2, 128, stride=32), :]
            im = in_ref[pl.ds(16 + u2, 128, stride=32), :]
            columns.append(jnp.concatenate([re, im], axis=0))
        high, low = split(jnp.concatenate(columns, axis=1))
        done = dot(table_ref[0], high) + dot(table_ref[1], high) + dot(table_ref[0], low)
        for index in range(2):
            for track in range(2):
                out_ref[pl.ds(group * 2048 + 8 * track + 2 * n + index, 128, stride=16), :] = done[
                    track * 128 : track * 128 + 128, index * 128 : index * 128 + 128
                ]
        return carry

    lax.fori_loop(0, 4, step, 0)


def place(group, in_ref, out_ref):
    def step(index, carry):
        vl = lax.div(index, 4)
        track = lax.rem(lax.div(index, 2), 2)
        high_u2 = lax.rem(index, 2)
        base = group * 2048 + vl * 16 + track * 8 + high_u2 * 4
        rows = [in_ref[pl.ds(base + low, 32, stride=64), :] for low in range(4)]
        turned = jnp.concatenate(rows, axis=0).T
        for u3 in range(16):
            column = pl.multiple_of((vl * 64 + u3 * 4 + group * 2 + high_u2) * 128, 128)
            out_ref[track, :, pl.ds(column, 128)] = turned[8 * u3 : 8 * u3 + 8, :]
        return carry

    lax.fori_loop(0, 16, step, 0)


def road_kernel(
    left_ref, right_ref, roughness_ref, waviness_ref, coherence_ref, row_hbm, lane_hbm, class_hbm, fold_hbm,
    profile_ref, factor_ref,
    row_ref, lane_ref, class_ref, fold_ref, sorted_ref, in1_ref, level_ref, twist_ref, high_ref, low_ref, part_ref,
    out2_ref, in2_ref, members_ref, total_ref, mine_ref, grams_ref, planes_ref, out3_ref, in3_ref,
    table_sem, own_sem, sems,
):
    me = lax.axis_index("len")
    plane = lax.axis_index("mem")
    other = {"len": lax.rem(me + 1, LEN)}
    above = {"mem": lax.rem(plane + 1, MEM)}
    loads = [
        pltpu.make_async_copy(source, target, table_sem.at[n])
        for n, (source, target) in enumerate(
            ((row_hbm, row_ref), (lane_hbm, lane_ref), (class_hbm, class_ref), (fold_hbm, fold_ref))
        )
    ]
    for load in loads:
        load.start()
    barrier = pltpu.get_barrier_semaphore()

    def greet(r, carry):
        pl.semaphore_signal(barrier, inc=1, device_id={"len": lax.rem(me + r, LEN)}, device_id_type=MESH)
        return carry

    lax.fori_loop(1, LEN, greet, 0)
    for r in range(1, MEM):
        pl.semaphore_signal(barrier, inc=1, device_id={"mem": lax.rem(plane + r, MEM)}, device_id_type=MESH)
    sort_phases(0, left_ref, sorted_ref)
    sort_phases(1, right_ref, sorted_ref)
    pl.semaphore_wait(barrier, LEN + MEM - 2)

    own = []
    for pair in range(2):
        for half in range(2):
            target = in1_ref.at[rows_at(pair * 2048 + me * 64 + half * 32, 32)]
            source = sorted_ref.at[rows_at(classes(me)[2 * pair + half] * 32, 32)]
            own.append(pltpu.make_async_copy(source, target, own_sem.at[2 * pair + half]))
            own[-1].start()
    for pair in range(2):
        for d in partners(me):
            for half in range(2):
                source = sorted_ref.at[rows_at(classes(d)[2 * pair + half] * 32, 32)]
                target = in1_ref.at[rows_at(pair * 2048 + me * 64 + half * 32, 32)]
                send(source, target, sems, pair, {"len": d})
    for pair in range(2):
        fill_levels(pair, me, roughness_ref, waviness_ref, coherence_ref, level_ref)
        fill_twist(pair, me, twist_ref)
    for load in loads:
        load.wait()
    for copy in own:
        copy.wait()

    own = []
    for pair in range(2):
        settle(in1_ref.at[pl.ds(0, 31 * 64)], sems, pair, other, 1)
        spectra(pair, in1_ref, level_ref, high_ref, low_ref)
        transforms(pair, me, high_ref, low_ref, row_ref, lane_ref, twist_ref, part_ref, out2_ref)
        span = pl.ds(64 * pair, 64)
        target = in2_ref.at[rows_at(me * 128 + 64 * pair, 64)]
        own.append(pltpu.make_async_copy(out2_ref.at[me, span], target, own_sem.at[4 + 2 * pair]))
        quarter = out2_ref.at[pl.ds(8 * plane, 8), span]
        target_mem = members_ref.at[plane, :, span]
        own.append(pltpu.make_async_copy(quarter, target_mem, own_sem.at[5 + 2 * pair]))
        own[-2].start()
        own[-1].start()
        for r in range(1, MEM):
            d = lax.rem(plane + r, MEM)
            send(out2_ref.at[pl.ds(8 * d, 8), span], target_mem, sems, 4 + pair, {"mem": d})
        for d in partners(me):
            send(out2_ref.at[d, span], target, sems, 2 + pair, {"len": d})
    for copy in own:
        copy.wait()

    for pair in range(2):
        settle(members_ref.at[pl.ds(0, 3), :, pl.ds(0, 64)], sems, 4 + pair, above, 1)
    mine_ref[...] = gram_part(members_ref, fold_ref, total_ref)
    grams_ref[me] = mine_ref[...]
    for d in partners(me):
        send(mine_ref, grams_ref.at[me], sems, 6, {"len": d})

    for pair in range(2):
        settle(in2_ref.at[pl.ds(0, 31 * 64)], sems, 2 + pair, other, 1)
    own = []
    for group in range(2):
        class_transform(group, in2_ref, class_ref, out3_ref)
        target = in3_ref.at[rows_at(group * 2048 + me * 64, 64)]
        own.append(
            pltpu.make_async_copy(out3_ref.at[rows_at(group * 2048 + me * 64, 64)], target, own_sem.at[8 + group])
        )
        own[-1].start()
        for d in partners(me):
            send(out3_ref.at[rows_at(group * 2048 + d * 64, 64)], target, sems, 7 + group, {"len": d})

    settle(grams_ref.at[pl.ds(0, 31)], sems, 6, other, 1)
    summed = lax.fori_loop(0, LEN, lambda n, total: total + grams_ref[n], jnp.zeros((8, LANES), F32))
    planes_ref[MEM] = summed
    planes_ref[plane] = summed
    for r in range(1, MEM):
        send(planes_ref.at[MEM], planes_ref.at[plane], sems, 9, {"mem": lax.rem(plane + r, MEM)})
    settle(planes_ref.at[pl.ds(0, 3)], sems, 9, above, 1)
    gram = planes_ref[0] + planes_ref[1] + planes_ref[2] + planes_ref[3]
    factor_ref[...] = upper_factor(gram)[:, :32]

    for copy in own:
        copy.wait()
    for group in range(2):
        settle(in3_ref.at[pl.ds(0, 31 * 64)], sems, 7 + group, other, 1)
        place(group, in3_ref, profile_ref)

    for pair in range(2):
        settle(in1_ref.at[pl.ds(0, 31 * 64)], sems, pair, other, 0)
        settle(in1_ref.at[pl.ds(0, 31 * 64)], sems, 2 + pair, other, 0)
        settle(members_ref.at[pl.ds(0, 3), :, pl.ds(0, 64)], sems, 4 + pair, above, 0)
        settle(in1_ref.at[pl.ds(0, 31 * 64)], sems, 7 + pair, other, 0)
    settle(grams_ref.at[pl.ds(0, 31)], sems, 6, other, 0)
    settle(planes_ref.at[pl.ds(0, 3)], sems, 9, above, 0)


def per_device(phase_left, phase_right, roughness, waviness, coherence):
    row_dft, lane_dft, class_dft, fold = tables()
    smem = pl.BlockSpec(memory_space=pltpu.SMEM)
    vmem = pl.BlockSpec(memory_space=pltpu.VMEM)
    hbm = pl.BlockSpec(memory_space=pl.ANY)
    return pl.pallas_call(
        road_kernel,
        out_shape=(jax.ShapeDtypeStruct((2, 8, 32768), F32), jax.ShapeDtypeStruct((32, 32), F32)),
        in_specs=[vmem, vmem, smem, smem, smem, hbm, hbm, hbm, hbm],
        out_specs=(vmem, vmem),
        scratch_shapes=[
            pltpu.VMEM(row_dft.shape, BF16),
            pltpu.VMEM(lane_dft.shape, BF16),
            pltpu.VMEM(class_dft.shape, BF16),
            pltpu.VMEM(fold.shape, F32),
            pltpu.VMEM((4096, LANES), F32),
            pltpu.VMEM((4096, LANES), F32),
            pltpu.VMEM((3, 2048, LANES), F32),
            pltpu.VMEM((2, 2048, LANES), F32),
            pltpu.VMEM((4, 2, 256, 256), BF16),
            pltpu.VMEM((4, 2, 256, 256), BF16),
            pltpu.VMEM((2, 2, 256, LANES), F32),
            pltpu.VMEM((LEN, 128, LANES), F32),
            pltpu.VMEM((4096, LANES), F32),
            pltpu.VMEM((MEM, 8, 128, LANES), F32),
            pltpu.VMEM((512, 512), F32),
            pltpu.VMEM((8, LANES), F32),
            pltpu.VMEM((LEN, 8, LANES), F32),
            pltpu.VMEM((MEM + 1, 8, LANES), F32),
            pltpu.VMEM((4096, LANES), F32),
            pltpu.VMEM((4096, LANES), F32),
            pltpu.SemaphoreType.DMA((4,)),
            pltpu.SemaphoreType.DMA((10,)),
            pltpu.SemaphoreType.DMA((2, 10)),
        ],
        compiler_params=pltpu.CompilerParams(
            collective_id=0, has_side_effects=True, vmem_limit_bytes=VMEM_LIMIT
        ),
        name="road_profiles",
    )(
        phase_left, phase_right, roughness, waviness, coherence,
        jnp.asarray(row_dft), jnp.asarray(lane_dft), jnp.asarray(class_dft), jnp.asarray(fold),
    )


def solution(mesh):
    placed = (P("mem", "len"), P("mem", "len"), P("mem"), P("mem"), P("mem"))
    return jax.shard_map(
        per_device,
        mesh=mesh,
        in_specs=placed,
        out_specs=(P(None, "mem", "len"), P()),
        check_vma=False,
    )
```

```python
import functools
import math

import jax
import jax.numpy as jnp
import ml_dtypes
import numpy as np
from jax import lax
from jax.experimental import pallas as pl
from jax.experimental.pallas import tpu as pltpu
from jax.sharding import PartitionSpec as P

ANCHOR = 64
POINTS = 1048576
LEN = 32
MEM = 4
ROWS = 128
LANES = 128
F32 = jnp.float32
BF16 = jnp.bfloat16
MESH = pl.DeviceIdType.MESH
VMEM_LIMIT = 40 * 1024 * 1024


def halves(table):
    table = np.asarray(table, np.float64)
    high = table.astype(np.float32).astype(ml_dtypes.bfloat16)
    low = (table - high.astype(np.float64)).astype(np.float32).astype(ml_dtypes.bfloat16)
    return np.stack([high, low])


def class_of():
    d = np.arange(LEN)
    rest = np.where(d == 0, 64, 128 - d)
    third = np.where(d == 0, 32, 64 - d)
    fourth = np.where(d == 0, 96, 64 + d)
    return np.stack([d, rest, third, fourth], axis=1)


@functools.lru_cache(None)
def tables():
    turn = 2.0 * math.pi
    w_row = np.arange(ROWS)
    w = w_row // 16 + 8 * (w_row % 16)
    r = np.arange(ROWS)
    row_tables = []
    for a in range(4):
        angle = turn * ((w[:, None] * r[None, :] % 128) / 128.0 + a * r[None, :] / 512.0)
        cos, sin = np.cos(angle), np.sin(angle)
        row_tables.append(halves(np.block([[cos, -sin], [sin, cos]])))
    row_dft = np.stack(row_tables)
    lane = np.arange(LANES)
    e, m = lane // 8, lane % 8
    same = (m[:, None] == m[None, :]).astype(np.float64)
    angle = turn * (e[:, None] * e[None, :] % 16) / 16.0
    cos, sin = 0.5 * same * np.cos(angle), 0.5 * same * np.sin(angle)
    lane_dft = halves(np.block([[cos, sin], [-sin, cos]]))
    v = np.arange(128)
    c = class_of().reshape(LEN, 2, 2).transpose(2, 0, 1).reshape(-1)
    angle = turn * (v[:, None] * c[None, :] % 128) / 128.0
    cos, sin = np.cos(angle), np.sin(angle)
    class_dft = halves(np.block([[cos, -sin], [sin, cos]]))
    index = np.arange(512)
    fold = np.zeros((512, LANES), np.float32)
    for a in range(4):
        fold[index, 32 * a + 8 * (index // 128) + index % 8] = 1.0
    return row_dft, lane_dft, class_dft, fold


@functools.lru_cache(None)
def sine_terms():
    h = np.cos(np.pi * (np.arange(4000) + 0.5) / 4000) * 1.575
    z = h * h
    sin = np.linalg.lstsq(np.stack([h ** (2 * n + 1) for n in range(6)], 1), np.sin(h), rcond=None)[0]
    cos = np.linalg.lstsq(np.stack([z**n for n in range(1, 7)], 1), np.cos(h) - 1.0, rcond=None)[0]
    return [float(x) for x in sin], [float(x) for x in cos]


def cos_sin(phase):
    sin_terms, cos_terms = sine_terms()
    half = phase * 0.5
    z = half * half
    s = jnp.full_like(z, sin_terms[-1])
    for term in sin_terms[-2::-1]:
        s = s * z + term
    s = s * half
    c = jnp.full_like(z, cos_terms[-1])
    for term in cos_terms[-2::-1]:
        c = c * z + term
    c = c * z + 1.0
    return 1.0 - 2.0 * (s * s), 2.0 * (s * c)


def split(x):
    high = x.astype(BF16)
    return high, (x - high.astype(F32)).astype(BF16)


def dot(a, b):
    return jnp.dot(a, b, preferred_element_type=F32)


def order():
    ring = lambda n: min(n, 4 - n)
    steps = [(dx, dy, dc) for dc in range(2) for dx in range(4) for dy in range(4) if (dx, dy, dc) != (0, 0, 0)]
    return sorted(steps, key=lambda s: (-ring(s[0]) - ring(s[1]), s[2]))


def partners(me):
    x, y, core = lax.div(me, 8), lax.rem(lax.div(me, 2), 4), lax.rem(me, 2)
    for dx, dy, dc in order():
        yield lax.rem(x + dx, 4) * 8 + lax.rem(y + dy, 4) * 2 + lax.rem(core + dc, 2)


def classes(d):
    first = d == 0
    return (d, jnp.where(first, 64, 128 - d), jnp.where(first, 32, 64 - d), jnp.where(first, 96, 64 + d))


def rows_at(start, size):
    return pl.ds(pl.multiple_of(start, 8), size)


def send(source, target, sems, index, device):
    pltpu.make_async_remote_copy(
        source, target, sems.at[0, index], sems.at[1, index], device_id=device, device_id_type=MESH
    ).start()


def settle(ref, sems, index, device, which):
    copy = pltpu.make_async_remote_copy(
        ref, ref, sems.at[0, index], sems.at[1, index], device_id=device, device_id_type=MESH
    )
    if which == 0:
        copy.wait_send()
    else:
        copy.wait_recv()


def unit_turn(numerator, size):
    cos, sin = cos_sin(numerator.astype(F32) * (2.0 * math.pi / size) - math.pi)
    return -cos, -sin


def sort_phases(index, ref, sorted_ref):
    def step(i, carry):
        tiles = [ref[:, pl.ds(pl.multiple_of(i * 2048 + e * 128, 128), 128)] for e in range(16)]
        sorted_ref[pl.ds(index * 16 + i, 128, stride=32), :] = jnp.concatenate(tiles, axis=0).T
        return carry

    lax.fori_loop(0, 16, step, 0, unroll=4)


def member_lanes(ref):
    lane = lax.rem(lax.broadcasted_iota(jnp.int32, (8, LANES), 1), 8)
    values = jnp.zeros((8, LANES), F32)
    for m in range(8):
        values = jnp.where(lane == m, ref[m], values)
    return values


def fill_levels(pair, me, roughness_ref, waviness_ref, coherence_ref, level_ref):
    waviness = member_lanes(waviness_ref)
    scale = jnp.sqrt(2.0 * member_lanes(roughness_ref) * (waviness - 1.0) * (1.0 / ANCHOR))
    exponent = -0.5 * waviness
    inverse = 1.0 / member_lanes(coherence_ref)
    row = lax.broadcasted_iota(jnp.int32, (8, LANES), 0)
    lane = lax.broadcasted_iota(jnp.int32, (8, LANES), 1)
    spread = row * 2048 + lax.div(lane, 8) * 128
    for half in range(2):
        offset = spread + classes(me)[2 * pair + half]

        def step(n, carry, half=half, offset=offset):
            freq = (offset + n * 16384).astype(F32)
            amplitude = scale * jnp.exp(exponent * jnp.log(freq * (1.0 / ANCHOR) + 1.0))
            ratio = freq * inverse
            square = ratio * ratio
            coherent = 1.0 / (1.0 + square)
            incoherent = ratio * jnp.sqrt(2.0 + square) * coherent
            rows = rows_at(pair * 1024 + half * 512 + n * 8, 8)
            level_ref[0, rows, :] = amplitude
            level_ref[1, rows, :] = amplitude * coherent
            level_ref[2, rows, :] = amplitude * incoherent
            return carry

        lax.fori_loop(0, 64, step, 0, unroll=4)


def fill_twist(pair, me, twist_ref):
    row = lax.broadcasted_iota(jnp.int32, (8, LANES), 0)
    lane = lax.broadcasted_iota(jnp.int32, (8, LANES), 1)
    for half in range(2):
        place = lax.div(lane, 8) * 128 + classes(me)[2 * pair + half]

        def step(n, carry, half=half, place=place):
            upper = lax.div(n, 16) + 4 * lax.rem(lax.div(n, 2), 8) + 32 * (lax.rem(n, 2) * 8 + row)
            cos, sin = unit_turn(lax.rem(upper * place, POINTS), POINTS)
            rows = rows_at(pair * 1024 + half * 512 + n * 8, 8)
            twist_ref[0, rows, :] = cos
            twist_ref[1, rows, :] = sin
            return carry

        lax.fori_loop(0, 64, step, 0, unroll=4)


def spectra(pair, in_ref, level_ref, high_ref, low_ref):
    def step(index, carry):
        half = lax.div(index, 8)
        low_p = lax.rem(index, 8)
        parts = []
        for q in range(4):
            p = 8 * q + low_p
            start = pair * 2048 + p * 64 + half * 32
            cos_left, sin_left = cos_sin(in_ref[rows_at(start, 16), :])
            cos_right, sin_right = cos_sin(in_ref[rows_at(start + 16, 16), :])
            rows = rows_at(pair * 1024 + half * 512 + p * 16, 16)
            amplitude, first, second = level_ref[0, rows, :], level_ref[1, rows, :], level_ref[2, rows, :]
            parts.append(
                (
                    amplitude * cos_left,
                    amplitude * sin_left,
                    first * cos_left + second * cos_right,
                    first * sin_left + second * sin_right,
                )
            )
        rows = pl.ds(pl.multiple_of(low_p * 16, 16), 16)
        imag_rows = pl.ds(pl.multiple_of(128 + low_p * 16, 16), 16)
        for track in range(2):
            re = [part[2 * track] for part in parts]
            im = [part[2 * track + 1] for part in parts]
            even_re, even_im = re[0] + re[2], im[0] + im[2]
            odd_re, odd_im = re[1] + re[3], im[1] + im[3]
            diff_re, diff_im = re[0] - re[2], im[0] - im[2]
            skew_re, skew_im = re[1] - re[3], im[1] - im[3]
            results = (
                (even_re + odd_re, even_im + odd_im),
                (diff_re - skew_im, diff_im + skew_re),
                (even_re - odd_re, even_im - odd_im),
                (diff_re + skew_im, diff_im - skew_re),
            )
            lanes = slice(track * 128, track * 128 + 128)
            for a, (x, y) in enumerate(results):
                high, low = split(x)
                high_ref[a, half, rows, lanes] = high
                low_ref[a, half, rows, lanes] = low
                high, low = split(y)
                high_ref[a, half, imag_rows, lanes] = high
                low_ref[a, half, imag_rows, lanes] = low
        return carry

    lax.fori_loop(0, 16, step, 0)


def transforms(pair, me, high_ref, low_ref, row_ref, lane_ref, twist_ref, part_ref, out_ref):
    is_first = me == 0
    lane = lax.div(lax.broadcasted_iota(jnp.int32, (1, LANES), 1), 8)
    turns = [unit_turn(lane * classes(me)[2 * pair + half], 2048) for half in range(2)]

    def step(a, carry):
        table_high, table_low = row_ref[a, 0], row_ref[a, 1]
        for half in range(2):
            high, low = high_ref[a, half], low_ref[a, half]
            partial = dot(table_high, high) + dot(table_low, high) + dot(table_high, low)
            rows = pl.ds(pl.multiple_of(pair * 1024 + half * 512 + a * 128, 128), 128)
            cos, sin = twist_ref[0, rows, :], twist_ref[1, rows, :]
            stacked = []
            for track in range(2):
                re = partial[:128, track * 128 : track * 128 + 128]
                im = partial[128:, track * 128 : track * 128 + 128]
                stacked.append(jnp.concatenate([re * cos - im * sin, re * sin + im * cos], axis=1))
            high, low = split(jnp.concatenate(stacked, axis=0))
            done = dot(high, lane_ref[0]) + dot(low, lane_ref[0]) + dot(high, lane_ref[1])
            cos, sin = turns[half]
            re, im = done[:, :128], done[:, 128:]
            part_ref[half, 0] = re * cos - im * sin
            part_ref[half, 1] = re * sin + im * cos
        re0, im0 = part_ref[0, 0, :128, :], part_ref[0, 1, :128, :]
        re1, im1 = part_ref[0, 0, 128:, :], part_ref[0, 1, 128:, :]
        mirror_re0, mirror_im0 = part_ref[1, 0, :128, :], part_ref[1, 1, :128, :]
        mirror_re1, mirror_im1 = part_ref[1, 0, 128:, :], part_ref[1, 1, 128:, :]
        sum_re0, sum_re1 = re0 + mirror_re0, re1 + mirror_re1
        gap_im0, gap_im1 = im0 - mirror_im0, im1 - mirror_im1
        packed = [
            [sum_re0 - gap_im1, gap_im0 + sum_re1],
            [sum_re0 + gap_im1, sum_re1 - gap_im0],
        ]
        if pair == 0:
            alone = [[re0 + re0, re1 + re1], [mirror_re0 + mirror_re0, mirror_re1 + mirror_re1]]
            packed = [[jnp.where(is_first, alone[n][x], packed[n][x]) for x in range(2)] for n in range(2)]
        for n in range(2):
            for x in range(2):
                for wl in range(8):
                    for g in range(2):
                        start = pair * 64 + g * 32 + n * 16 + x * 8
                        out_ref[4 * wl + a, start : start + 8, :] = packed[n][x][
                            wl * 16 + g * 8 : wl * 16 + g * 8 + 8, :
                        ]
        return carry

    lax.fori_loop(0, 4, step, 0)


def gram_part(members_ref, fold_ref, total_ref):
    total_ref[...] = jnp.zeros_like(total_ref)
    product = functools.partial(
        lax.dot_general, dimension_numbers=(((0,), (0,)), ((), ())), preferred_element_type=F32
    )

    def step(n, carry):
        rows = [members_ref[z, pl.ds(2 * n, 2)].reshape(256, LANES) for z in range(MEM)]
        high, low = split(jnp.concatenate(rows, axis=1))
        total_ref[...] += product(high, high) + product(low, high) + product(high, low)
        return carry

    lax.fori_loop(0, 4, step, 0)
    row = lax.broadcasted_iota(jnp.int32, (512, 512), 0)
    column = lax.broadcasted_iota(jnp.int32, (512, 512), 1)
    same = lax.rem(lax.div(row, 8), 16) == lax.rem(lax.div(column, 8), 16)
    kept = jnp.where(same, total_ref[...], 0.0)
    right = jnp.dot(kept, fold_ref[...], preferred_element_type=F32, precision=lax.Precision.HIGHEST)
    row = lax.broadcasted_iota(jnp.int32, (512, LANES), 0)
    lane = lax.broadcasted_iota(jnp.int32, (512, LANES), 1)
    right = jnp.where(lax.div(row, 128) == lax.div(lane, 32), right, 0.0)
    return jnp.sum(right.reshape(64, 8, LANES), axis=0) * (128.0 / (2.0 * POINTS))


def upper_factor(gram):
    row = lax.broadcasted_iota(jnp.int32, (32, LANES), 0)
    lane = lax.broadcasted_iota(jnp.int32, (32, LANES), 1)
    tall = jnp.concatenate([gram] * 4, axis=0)
    tall = jnp.where(lax.div(row, 8) == lax.div(lane, 32), tall, 0.0)
    pick_row = lax.broadcasted_iota(jnp.int32, (LANES, LANES), 0)
    pick_lane = lax.broadcasted_iota(jnp.int32, (LANES, LANES), 1)
    pick = jnp.where(lax.rem(pick_row, 32) == pick_lane, 1.0, 0.0)
    matrix = jnp.dot(tall, pick, preferred_element_type=F32, precision=lax.Precision.HIGHEST)

    def step(n, carry):
        rest, upper = carry
        line = jnp.sum(jnp.where(row == n, rest, 0.0), axis=0, keepdims=True)
        column = jnp.sum(jnp.where(lane == n, rest, 0.0), axis=1, keepdims=True)
        pivot = jnp.sum(jnp.where(lane[0:1] == n, line, 0.0), axis=1, keepdims=True)
        line = jnp.where(lane[0:1] >= n, line / jnp.sqrt(pivot), 0.0)
        column = column / jnp.sqrt(pivot)
        return rest - column * line, jnp.where(row == n, line, upper)

    return lax.fori_loop(0, 32, step, (matrix, jnp.zeros_like(matrix)))[1]


def class_transform(group, in_ref, table_ref, out_ref):
    for n in range(2):
        columns = []
        for index in range(2):
            u2 = 4 * group + 2 * n + index
            start = (u2 // 8) * 32 + u2 % 8
            parts = [in_ref[pl.ds(start + 8 * x + 16 * half, 64, stride=64), :] for x in range(2) for half in range(2)]
            columns.append(jnp.concatenate(parts, axis=0))
        high, low = split(jnp.concatenate(columns, axis=1))
        done = dot(table_ref[0], high) + dot(table_ref[1], high) + dot(table_ref[0], low)
        for index in range(2):
            for track in range(2):
                out_ref[pl.ds(group * 1024 + 4 * track + 2 * n + index, 128, stride=8), :] = done[
                    track * 128 : track * 128 + 128, index * 128 : index * 128 + 128
                ]


def place(group, in_ref, out_ref):
    def step(index, carry):
        vl = lax.div(index, 2)
        track = lax.rem(index, 2)
        base = group * 1024 + vl * 8 + track * 4
        rows = [in_ref[pl.ds(base + low, 32, stride=32), :] for low in range(4)]
        turned = jnp.concatenate(rows, axis=0).T
        for u3 in range(16):
            column = pl.multiple_of((vl * 64 + u3 * 4 + group) * 128, 128)
            out_ref[track, :, pl.ds(column, 128)] = turned[8 * u3 : 8 * u3 + 8, :]
        return carry

    lax.fori_loop(0, 8, step, 0, unroll=2)


def road_kernel(
    left_hbm, right_hbm, roughness_ref, waviness_ref, coherence_ref, row_hbm, lane_hbm, class_hbm, fold_hbm,
    profile_ref, factor_ref,
    left_ref, right_ref, row_ref, lane_ref, class_ref, fold_ref, sorted_ref, in1_ref, level_ref, twist_ref, high_ref, low_ref, part_ref,
    out2_ref, in2_ref, members_ref, total_ref, mine_ref, grams_ref, planes_ref, out3_ref, in3_ref,
    table_sem, own_sem, sems,
):
    me = lax.axis_index("len")
    plane = lax.axis_index("mem")
    other = {"len": lax.rem(me + 1, LEN)}
    above = {"mem": lax.rem(plane + 1, MEM)}
    pieces = [(left_hbm, left_ref), (right_hbm, right_ref)]
    pieces += [(row_hbm, row_ref), (lane_hbm, lane_ref), (class_hbm, class_ref), (fold_hbm, fold_ref)]
    loads = [pltpu.make_async_copy(source, target, table_sem.at[n]) for n, (source, target) in enumerate(pieces)]
    for load in loads:
        load.start()
    barrier = pltpu.get_barrier_semaphore()

    def greet(r, carry):
        pl.semaphore_signal(barrier, inc=1, device_id={"len": lax.rem(me + r, LEN)}, device_id_type=MESH)
        return carry

    lax.fori_loop(1, LEN, greet, 0)
    for r in range(1, MEM):
        pl.semaphore_signal(barrier, inc=1, device_id={"mem": lax.rem(plane + r, MEM)}, device_id_type=MESH)
    loads[0].wait()
    sort_phases(0, left_ref, sorted_ref)
    loads[1].wait()
    sort_phases(1, right_ref, sorted_ref)
    pl.semaphore_wait(barrier, LEN + MEM - 2)

    own = []
    for pair in range(2):
        for half in range(2):
            target = in1_ref.at[rows_at(pair * 2048 + me * 64 + half * 32, 32)]
            source = sorted_ref.at[rows_at(classes(me)[2 * pair + half] * 32, 32)]
            own.append(pltpu.make_async_copy(source, target, own_sem.at[2 * pair + half]))
            own[-1].start()
    for pair in range(2):
        for d in partners(me):
            for half in range(2):
                source = sorted_ref.at[rows_at(classes(d)[2 * pair + half] * 32, 32)]
                target = in1_ref.at[rows_at(pair * 2048 + me * 64 + half * 32, 32)]
                send(source, target, sems, pair, {"len": d})
    for pair in range(2):
        fill_levels(pair, me, roughness_ref, waviness_ref, coherence_ref, level_ref)
        fill_twist(pair, me, twist_ref)
    for load in loads[2:]:
        load.wait()
    for copy in own:
        copy.wait()

    own = []
    for pair in range(2):
        settle(in1_ref.at[pl.ds(0, 31 * 64)], sems, pair, other, 1)
        spectra(pair, in1_ref, level_ref, high_ref, low_ref)
        transforms(pair, me, high_ref, low_ref, row_ref, lane_ref, twist_ref, part_ref, out2_ref)
        span = pl.ds(64 * pair, 64)
        target = in2_ref.at[rows_at(me * 128 + 64 * pair, 64)]
        own.append(pltpu.make_async_copy(out2_ref.at[me, span], target, own_sem.at[4 + 2 * pair]))
        quarter = out2_ref.at[pl.ds(8 * plane, 8), span]
        target_mem = members_ref.at[plane, :, span]
        own.append(pltpu.make_async_copy(quarter, target_mem, own_sem.at[5 + 2 * pair]))
        own[-2].start()
        own[-1].start()
        for r in range(1, MEM):
            d = lax.rem(plane + r, MEM)
            send(out2_ref.at[pl.ds(8 * d, 8), span], target_mem, sems, 4 + pair, {"mem": d})
        for start, size, sem in ((0, 64, 2),) if pair == 0 else ((64, 32, 3), (96, 32, 10)):
            for d in partners(me):
                target = in2_ref.at[rows_at(me * 128 + start, size)]
                send(out2_ref.at[d, pl.ds(start, size)], target, sems, sem, {"len": d})
    for copy in own:
        copy.wait()

    for pair in range(2):
        settle(members_ref.at[pl.ds(0, 3), :, pl.ds(0, 64)], sems, 4 + pair, above, 1)
    mine_ref[...] = gram_part(members_ref, fold_ref, total_ref)
    grams_ref[me] = mine_ref[...]
    for d in partners(me):
        send(mine_ref, grams_ref.at[me], sems, 6, {"len": d})

    settle(in2_ref.at[pl.ds(0, 31 * 64)], sems, 2, other, 1)
    own = []
    for group in range(4):
        if group % 2 == 0:
            settle(in2_ref.at[pl.ds(0, 31 * 32)], sems, (3, 10)[group // 2], other, 1)
        class_transform(group, in2_ref, class_ref, out3_ref)
        target = in3_ref.at[rows_at(group * 1024 + me * 32, 32)]
        mine = out3_ref.at[rows_at(group * 1024 + me * 32, 32)]
        own.append(pltpu.make_async_copy(mine, target, own_sem.at[8 + group]))
        own[-1].start()
        for d in partners(me):
            send(out3_ref.at[rows_at(group * 1024 + d * 32, 32)], target, sems, 11 + group, {"len": d})

    settle(grams_ref.at[pl.ds(0, 31)], sems, 6, other, 1)
    summed = lax.fori_loop(0, LEN, lambda n, total: total + grams_ref[n], jnp.zeros((8, LANES), F32))
    planes_ref[MEM] = summed
    planes_ref[plane] = summed
    for r in range(1, MEM):
        send(planes_ref.at[MEM], planes_ref.at[plane], sems, 9, {"mem": lax.rem(plane + r, MEM)})
    settle(planes_ref.at[pl.ds(0, 3)], sems, 9, above, 1)
    gram = planes_ref[0] + planes_ref[1] + planes_ref[2] + planes_ref[3]
    factor_ref[...] = upper_factor(gram)[:, :32]

    for copy in own:
        copy.wait()
    for group in range(4):
        settle(in3_ref.at[pl.ds(0, 31 * 32)], sems, 11 + group, other, 1)
        place(group, in3_ref, profile_ref)

    for sem, ref in ((0, in1_ref), (1, in1_ref), (2, in1_ref)):
        settle(ref.at[pl.ds(0, 31 * 64)], sems, sem, other, 0)
    for sem in (3, 10, 11, 12, 13, 14):
        settle(in1_ref.at[pl.ds(0, 31 * 32)], sems, sem, other, 0)
    for pair in range(2):
        settle(members_ref.at[pl.ds(0, 3), :, pl.ds(0, 64)], sems, 4 + pair, above, 0)
    settle(grams_ref.at[pl.ds(0, 31)], sems, 6, other, 0)
    settle(planes_ref.at[pl.ds(0, 3)], sems, 9, above, 0)


def hand_over_kernel(profile_in, factor_in, profile_out, factor_out, sems):
    copies = [
        pltpu.make_async_copy(profile_in, profile_out, sems.at[0]),
        pltpu.make_async_copy(factor_in, factor_out, sems.at[1]),
    ]
    for copy in copies:
        copy.start()
    for copy in copies:
        copy.wait()


def hand_over(profile, factor):
    vmem = pl.BlockSpec(memory_space=pltpu.VMEM)
    hbm = pl.BlockSpec(memory_space=pl.ANY)
    return pl.pallas_call(
        hand_over_kernel,
        out_shape=(jax.ShapeDtypeStruct(profile.shape, F32), jax.ShapeDtypeStruct(factor.shape, F32)),
        in_specs=[vmem, vmem],
        out_specs=(hbm, hbm),
        scratch_shapes=[pltpu.SemaphoreType.DMA((2,))],
        compiler_params=pltpu.CompilerParams(vmem_limit_bytes=8 * 1024 * 1024),
        name="hand_over",
    )(profile, factor)


def pinned(array):
    return pltpu.with_memory_space_constraint(array, pltpu.HBM)


def per_device(phase_left, phase_right, roughness, waviness, coherence):
    row_dft, lane_dft, class_dft, fold = tables()
    smem = pl.BlockSpec(memory_space=pltpu.SMEM)
    vmem = pl.BlockSpec(memory_space=pltpu.VMEM)
    hbm = pl.BlockSpec(memory_space=pltpu.HBM)
    profile, factor = pl.pallas_call(
        road_kernel,
        out_shape=(jax.ShapeDtypeStruct((2, 8, 32768), F32), jax.ShapeDtypeStruct((32, 32), F32)),
        in_specs=[hbm, hbm, smem, smem, smem, hbm, hbm, hbm, hbm],
        out_specs=(vmem, vmem),
        scratch_shapes=[
            pltpu.VMEM((8, 32768), F32),
            pltpu.VMEM((8, 32768), F32),
            pltpu.VMEM(row_dft.shape, BF16),
            pltpu.VMEM(lane_dft.shape, BF16),
            pltpu.VMEM(class_dft.shape, BF16),
            pltpu.VMEM(fold.shape, F32),
            pltpu.VMEM((4096, LANES), F32),
            pltpu.VMEM((4096, LANES), F32),
            pltpu.VMEM((3, 2048, LANES), F32),
            pltpu.VMEM((2, 2048, LANES), F32),
            pltpu.VMEM((4, 2, 256, 256), BF16),
            pltpu.VMEM((4, 2, 256, 256), BF16),
            pltpu.VMEM((2, 2, 256, LANES), F32),
            pltpu.VMEM((LEN, 128, LANES), F32),
            pltpu.VMEM((4096, LANES), F32),
            pltpu.VMEM((MEM, 8, 128, LANES), F32),
            pltpu.VMEM((512, 512), F32),
            pltpu.VMEM((8, LANES), F32),
            pltpu.VMEM((LEN, 8, LANES), F32),
            pltpu.VMEM((MEM + 1, 8, LANES), F32),
            pltpu.VMEM((4096, LANES), F32),
            pltpu.VMEM((4096, LANES), F32),
            pltpu.SemaphoreType.DMA((6,)),
            pltpu.SemaphoreType.DMA((12,)),
            pltpu.SemaphoreType.DMA((2, 15)),
        ],
        compiler_params=pltpu.CompilerParams(
            collective_id=0, has_side_effects=True, vmem_limit_bytes=VMEM_LIMIT
        ),
        name="road_profiles",
    )(
        *(pinned(array) for array in (phase_left, phase_right, roughness, waviness, coherence)),
        *(pinned(jnp.asarray(table)) for table in (row_dft, lane_dft, class_dft, fold)),
    )
    return hand_over(profile, factor)


def solution(mesh):
    placed = (P("mem", "len"), P("mem", "len"), P("mem"), P("mem"), P("mem"))
    return jax.shard_map(
        per_device,
        mesh=mesh,
        in_specs=placed,
        out_specs=(P(None, "mem", "len"), P()),
        check_vma=False,
    )
```

```python
import functools
import math

import jax
import jax.numpy as jnp
import ml_dtypes
import numpy as np
from jax import lax
from jax.experimental import pallas as pl
from jax.experimental.pallas import tpu as pltpu
from jax.sharding import PartitionSpec as P

ANCHOR = 64
POINTS = 1048576
LEN = 32
MEM = 4
ROWS = 128
LANES = 128
F32 = jnp.float32
BF16 = jnp.bfloat16
MESH = pl.DeviceIdType.MESH
VMEM_LIMIT = 40 * 1024 * 1024


def halves(table):
    table = np.asarray(table, np.float64)
    high = table.astype(np.float32).astype(ml_dtypes.bfloat16)
    low = (table - high.astype(np.float64)).astype(np.float32).astype(ml_dtypes.bfloat16)
    return np.stack([high, low])


def class_of():
    d = np.arange(LEN)
    rest = np.where(d == 0, 64, 128 - d)
    third = np.where(d == 0, 32, 64 - d)
    fourth = np.where(d == 0, 96, 64 + d)
    return np.stack([d, rest, third, fourth], axis=1)


@functools.lru_cache(None)
def tables():
    turn = 2.0 * math.pi
    w_row = np.arange(ROWS)
    w = w_row // 16 + 8 * (w_row % 16)
    r = np.arange(ROWS)
    row_tables = []
    for a in range(4):
        angle = turn * ((w[:, None] * r[None, :] % 128) / 128.0 + a * r[None, :] / 512.0)
        cos, sin = np.cos(angle), np.sin(angle)
        row_tables.append(halves(np.block([[cos, -sin], [sin, cos]])))
    row_dft = np.stack(row_tables)
    lane = np.arange(LANES)
    e, m = lane // 8, lane % 8
    same = (m[:, None] == m[None, :]).astype(np.float64)
    angle = turn * (e[:, None] * e[None, :] % 16) / 16.0
    cos, sin = 0.5 * same * np.cos(angle), 0.5 * same * np.sin(angle)
    lane_dft = halves(np.block([[cos, sin], [-sin, cos]]))
    v = np.arange(128)
    c = class_of().reshape(LEN, 2, 2).transpose(2, 0, 1).reshape(-1)
    angle = turn * (v[:, None] * c[None, :] % 128) / 128.0
    cos, sin = np.cos(angle), np.sin(angle)
    class_dft = halves(np.block([[cos, -sin], [sin, cos]]))
    index = np.arange(512)
    fold = np.zeros((512, LANES), np.float32)
    for a in range(4):
        fold[index, 32 * a + 8 * (index // 128) + index % 8] = 1.0
    return row_dft, lane_dft, class_dft, fold


@functools.lru_cache(None)
def sine_terms():
    h = np.cos(np.pi * (np.arange(4000) + 0.5) / 4000) * 1.575
    z = h * h
    sin = np.linalg.lstsq(np.stack([h ** (2 * n + 1) for n in range(6)], 1), np.sin(h), rcond=None)[0]
    cos = np.linalg.lstsq(np.stack([z**n for n in range(1, 7)], 1), np.cos(h) - 1.0, rcond=None)[0]
    return [float(x) for x in sin], [float(x) for x in cos]


def cos_sin(phase):
    sin_terms, cos_terms = sine_terms()
    half = phase * 0.5
    z = half * half
    s = jnp.full_like(z, sin_terms[-1])
    for term in sin_terms[-2::-1]:
        s = s * z + term
    s = s * half
    c = jnp.full_like(z, cos_terms[-1])
    for term in cos_terms[-2::-1]:
        c = c * z + term
    c = c * z + 1.0
    return 1.0 - 2.0 * (s * s), 2.0 * (s * c)


def split(x):
    high = x.astype(BF16)
    return high, (x - high.astype(F32)).astype(BF16)


def dot(a, b):
    return jnp.dot(a, b, preferred_element_type=F32)


def order():
    chips = [(2, 2), (1, 2), (2, 1), (3, 2), (2, 3), (0, 2), (2, 0), (1, 1), (3, 3), (1, 3), (3, 1)]
    chips += [(0, 1), (1, 0), (0, 3), (3, 0)]
    return [(dx, dy, dc) for dc in range(2) for dx, dy in chips] + [(0, 0, 1)]


def partners(me):
    x, y, core = lax.div(me, 8), lax.rem(lax.div(me, 2), 4), lax.rem(me, 2)
    for dx, dy, dc in order():
        yield lax.rem(x + dx, 4) * 8 + lax.rem(y + dy, 4) * 2 + lax.rem(core + dc, 2)


def classes(d):
    first = d == 0
    return (d, jnp.where(first, 64, 128 - d), jnp.where(first, 32, 64 - d), jnp.where(first, 96, 64 + d))


def rows_at(start, size):
    return pl.ds(pl.multiple_of(start, 8), size)


def send(source, target, sems, index, device):
    pltpu.make_async_remote_copy(
        source, target, sems.at[0, index], sems.at[1, index], device_id=device, device_id_type=MESH
    ).start()


def settle(ref, sems, index, device, which):
    copy = pltpu.make_async_remote_copy(
        ref, ref, sems.at[0, index], sems.at[1, index], device_id=device, device_id_type=MESH
    )
    if which == 0:
        copy.wait_send()
    else:
        copy.wait_recv()


def unit_turn(numerator, size):
    cos, sin = cos_sin(numerator.astype(F32) * (2.0 * math.pi / size) - math.pi)
    return -cos, -sin


def sort_phases(index, ref, sorted_ref):
    def step(i, carry):
        tiles = [ref[:, pl.ds(pl.multiple_of(i * 2048 + e * 128, 128), 128)] for e in range(16)]
        sorted_ref[pl.ds(index * 16 + i, 128, stride=32), :] = jnp.concatenate(tiles, axis=0).T
        return carry

    lax.fori_loop(0, 16, step, 0, unroll=4)


def member_lanes(ref):
    lane = lax.rem(lax.broadcasted_iota(jnp.int32, (8, LANES), 1), 8)
    values = jnp.zeros((8, LANES), F32)
    for m in range(8):
        values = jnp.where(lane == m, ref[m], values)
    return values


def fill_levels(pair, me, roughness_ref, waviness_ref, coherence_ref, level_ref):
    waviness = member_lanes(waviness_ref)
    scale = jnp.sqrt(2.0 * member_lanes(roughness_ref) * (waviness - 1.0) * (1.0 / ANCHOR))
    exponent = -0.5 * waviness
    inverse = 1.0 / member_lanes(coherence_ref)
    row = lax.broadcasted_iota(jnp.int32, (8, LANES), 0)
    lane = lax.broadcasted_iota(jnp.int32, (8, LANES), 1)
    spread = row * 2048 + lax.div(lane, 8) * 128
    for half in range(2):
        offset = spread + classes(me)[2 * pair + half]

        def step(n, carry, half=half, offset=offset):
            freq = (offset + n * 16384).astype(F32)
            amplitude = scale * jnp.exp(exponent * jnp.log(freq * (1.0 / ANCHOR) + 1.0))
            ratio = freq * inverse
            square = ratio * ratio
            coherent = 1.0 / (1.0 + square)
            incoherent = ratio * jnp.sqrt(2.0 + square) * coherent
            rows = rows_at(pair * 1024 + half * 512 + n * 8, 8)
            level_ref[0, rows, :] = amplitude
            level_ref[1, rows, :] = amplitude * coherent
            level_ref[2, rows, :] = amplitude * incoherent
            return carry

        lax.fori_loop(0, 64, step, 0, unroll=4)


def fill_twist(pair, me, twist_ref):
    row = lax.broadcasted_iota(jnp.int32, (8, LANES), 0)
    lane = lax.broadcasted_iota(jnp.int32, (8, LANES), 1)
    for half in range(2):
        place = lax.div(lane, 8) * 128 + classes(me)[2 * pair + half]

        def step(n, carry, half=half, place=place):
            upper = lax.div(n, 16) + 4 * lax.rem(lax.div(n, 2), 8) + 32 * (lax.rem(n, 2) * 8 + row)
            cos, sin = unit_turn(lax.rem(upper * place, POINTS), POINTS)
            rows = rows_at(pair * 1024 + half * 512 + n * 8, 8)
            twist_ref[0, rows, :] = cos
            twist_ref[1, rows, :] = sin
            return carry

        lax.fori_loop(0, 64, step, 0, unroll=4)


def spectra(pair, in_ref, level_ref, high_ref, low_ref):
    def step(index, carry):
        half = lax.div(index, 8)
        low_p = lax.rem(index, 8)
        parts = []
        for q in range(4):
            p = 8 * q + low_p
            start = pair * 2048 + p * 64 + half * 32
            cos_left, sin_left = cos_sin(in_ref[rows_at(start, 16), :])
            cos_right, sin_right = cos_sin(in_ref[rows_at(start + 16, 16), :])
            rows = rows_at(pair * 1024 + half * 512 + p * 16, 16)
            amplitude, first, second = level_ref[0, rows, :], level_ref[1, rows, :], level_ref[2, rows, :]
            parts.append(
                (
                    amplitude * cos_left,
                    amplitude * sin_left,
                    first * cos_left + second * cos_right,
                    first * sin_left + second * sin_right,
                )
            )
        rows = pl.ds(pl.multiple_of(low_p * 16, 16), 16)
        imag_rows = pl.ds(pl.multiple_of(128 + low_p * 16, 16), 16)
        for track in range(2):
            re = [part[2 * track] for part in parts]
            im = [part[2 * track + 1] for part in parts]
            even_re, even_im = re[0] + re[2], im[0] + im[2]
            odd_re, odd_im = re[1] + re[3], im[1] + im[3]
            diff_re, diff_im = re[0] - re[2], im[0] - im[2]
            skew_re, skew_im = re[1] - re[3], im[1] - im[3]
            results = (
                (even_re + odd_re, even_im + odd_im),
                (diff_re - skew_im, diff_im + skew_re),
                (even_re - odd_re, even_im - odd_im),
                (diff_re + skew_im, diff_im - skew_re),
            )
            lanes = slice(track * 128, track * 128 + 128)
            for a, (x, y) in enumerate(results):
                high, low = split(x)
                high_ref[a, half, rows, lanes] = high
                low_ref[a, half, rows, lanes] = low
                high, low = split(y)
                high_ref[a, half, imag_rows, lanes] = high
                low_ref[a, half, imag_rows, lanes] = low
        return carry

    lax.fori_loop(0, 16, step, 0)


def transforms(pair, me, high_ref, low_ref, row_ref, lane_ref, twist_ref, part_ref, out_ref):
    is_first = me == 0
    lane = lax.div(lax.broadcasted_iota(jnp.int32, (1, LANES), 1), 8)
    turns = [unit_turn(lane * classes(me)[2 * pair + half], 2048) for half in range(2)]

    def step(a, carry):
        table_high, table_low = row_ref[a, 0], row_ref[a, 1]
        for half in range(2):
            high, low = high_ref[a, half], low_ref[a, half]
            partial = dot(table_high, high) + dot(table_low, high) + dot(table_high, low)
            rows = pl.ds(pl.multiple_of(pair * 1024 + half * 512 + a * 128, 128), 128)
            cos, sin = twist_ref[0, rows, :], twist_ref[1, rows, :]
            stacked = []
            for track in range(2):
                re = partial[:128, track * 128 : track * 128 + 128]
                im = partial[128:, track * 128 : track * 128 + 128]
                stacked.append(jnp.concatenate([re * cos - im * sin, re * sin + im * cos], axis=1))
            high, low = split(jnp.concatenate(stacked, axis=0))
            done = dot(high, lane_ref[0]) + dot(low, lane_ref[0]) + dot(high, lane_ref[1])
            cos, sin = turns[half]
            re, im = done[:, :128], done[:, 128:]
            part_ref[half, 0] = re * cos - im * sin
            part_ref[half, 1] = re * sin + im * cos
        re0, im0 = part_ref[0, 0, :128, :], part_ref[0, 1, :128, :]
        re1, im1 = part_ref[0, 0, 128:, :], part_ref[0, 1, 128:, :]
        mirror_re0, mirror_im0 = part_ref[1, 0, :128, :], part_ref[1, 1, :128, :]
        mirror_re1, mirror_im1 = part_ref[1, 0, 128:, :], part_ref[1, 1, 128:, :]
        sum_re0, sum_re1 = re0 + mirror_re0, re1 + mirror_re1
        gap_im0, gap_im1 = im0 - mirror_im0, im1 - mirror_im1
        packed = [
            [sum_re0 - gap_im1, gap_im0 + sum_re1],
            [sum_re0 + gap_im1, sum_re1 - gap_im0],
        ]
        if pair == 0:
            alone = [[re0 + re0, re1 + re1], [mirror_re0 + mirror_re0, mirror_re1 + mirror_re1]]
            packed = [[jnp.where(is_first, alone[n][x], packed[n][x]) for x in range(2)] for n in range(2)]
        for n in range(2):
            for x in range(2):
                for wl in range(8):
                    for g in range(2):
                        start = pair * 64 + g * 32 + n * 16 + x * 8
                        out_ref[4 * wl + a, start : start + 8, :] = packed[n][x][
                            wl * 16 + g * 8 : wl * 16 + g * 8 + 8, :
                        ]
        return carry

    lax.fori_loop(0, 4, step, 0)


def gram_half(pair, members_ref, total_ref):
    product = functools.partial(
        lax.dot_general, dimension_numbers=(((0,), (0,)), ((), ())), preferred_element_type=F32
    )

    def step(n):
        span = pl.ds(64 * pair, 64)
        rows = [members_ref[z, pl.ds(4 * n, 4), span].reshape(256, LANES) for z in range(MEM)]
        high, low = split(jnp.concatenate(rows, axis=1))
        part = product(high, high) + product(low, high) + product(high, low)
        total_ref[...] = part if pair == 0 and n == 0 else total_ref[...] + part

    step(0)
    step(1)


def gram_part(fold_ref, total_ref):
    row = lax.broadcasted_iota(jnp.int32, (512, 512), 0)
    column = lax.broadcasted_iota(jnp.int32, (512, 512), 1)
    same = lax.rem(lax.div(row, 8), 16) == lax.rem(lax.div(column, 8), 16)
    kept = jnp.where(same, total_ref[...], 0.0)
    right = jnp.dot(kept, fold_ref[...], preferred_element_type=F32, precision=lax.Precision.HIGHEST)
    row = lax.broadcasted_iota(jnp.int32, (512, LANES), 0)
    lane = lax.broadcasted_iota(jnp.int32, (512, LANES), 1)
    right = jnp.where(lax.div(row, 128) == lax.div(lane, 32), right, 0.0)
    return jnp.sum(right.reshape(64, 8, LANES), axis=0) * (128.0 / (2.0 * POINTS))


def upper_factor(gram):
    row = lax.broadcasted_iota(jnp.int32, (32, LANES), 0)
    lane = lax.broadcasted_iota(jnp.int32, (32, LANES), 1)
    tall = jnp.concatenate([gram] * 4, axis=0)
    tall = jnp.where(lax.div(row, 8) == lax.div(lane, 32), tall, 0.0)
    pick_row = lax.broadcasted_iota(jnp.int32, (LANES, LANES), 0)
    pick_lane = lax.broadcasted_iota(jnp.int32, (LANES, LANES), 1)
    pick = jnp.where(lax.rem(pick_row, 32) == pick_lane, 1.0, 0.0)
    matrix = jnp.dot(tall, pick, preferred_element_type=F32, precision=lax.Precision.HIGHEST)

    def step(n, carry):
        rest, upper = carry
        column = jnp.sum(jnp.where(lane == n, rest, 0.0), axis=1, keepdims=True)
        line = jnp.sum(jnp.where(row == n, rest, 0.0), axis=0, keepdims=True)
        pivot = jnp.sum(jnp.where(row[:, 0:1] == n, column, 0.0), axis=0, keepdims=True)
        inverse = 1.0 / jnp.sqrt(pivot)
        line = jnp.where(lane[0:1] >= n, line * inverse, 0.0)
        column = column * inverse
        return rest - column * line, jnp.where(row == n, line, upper)

    return lax.fori_loop(0, 32, step, (matrix, jnp.zeros_like(matrix)))[1]


def class_transform(group, in_ref, table_ref, out_ref):
    for n in range(2):
        columns = []
        for index in range(2):
            u2 = 4 * group + 2 * n + index
            start = (u2 // 8) * 32 + u2 % 8
            parts = [in_ref[pl.ds(start + 8 * x + 16 * half, 64, stride=64), :] for x in range(2) for half in range(2)]
            columns.append(jnp.concatenate(parts, axis=0))
        high, low = split(jnp.concatenate(columns, axis=1))
        done = dot(table_ref[0], high) + dot(table_ref[1], high) + dot(table_ref[0], low)
        for index in range(2):
            for track in range(2):
                out_ref[pl.ds(group * 1024 + 4 * track + 2 * n + index, 128, stride=8), :] = done[
                    track * 128 : track * 128 + 128, index * 128 : index * 128 + 128
                ]


def place(group, in_ref, out_ref):
    def step(index, carry):
        vl = lax.div(index, 2)
        track = lax.rem(index, 2)
        base = group * 1024 + vl * 8 + track * 4
        rows = [in_ref[pl.ds(base + low, 32, stride=32), :] for low in range(4)]
        turned = jnp.concatenate(rows, axis=0).T
        for u3 in range(16):
            column = pl.multiple_of((vl * 64 + u3 * 4 + group) * 128, 128)
            out_ref[track, :, pl.ds(column, 128)] = turned[8 * u3 : 8 * u3 + 8, :]
        return carry

    lax.fori_loop(0, 8, step, 0, unroll=2)


def road_kernel(
    left_hbm, right_hbm, roughness_ref, waviness_ref, coherence_ref, row_hbm, lane_hbm, class_hbm, fold_hbm,
    profile_ref, factor_ref,
    left_ref, right_ref, row_ref, lane_ref, class_ref, fold_ref, sorted_ref, in1_ref, level_ref, twist_ref, high_ref, low_ref, part_ref,
    out2_ref, in2_ref, members_ref, total_ref, mine_ref, grams_ref, planes_ref, out3_ref, in3_ref,
    table_sem, own_sem, sems,
):
    me = lax.axis_index("len")
    plane = lax.axis_index("mem")
    other = {"len": lax.rem(me + 1, LEN)}
    above = {"mem": lax.rem(plane + 1, MEM)}
    pieces = [(left_hbm, left_ref), (right_hbm, right_ref)]
    pieces += [(row_hbm, row_ref), (lane_hbm, lane_ref), (class_hbm, class_ref), (fold_hbm, fold_ref)]
    loads = [pltpu.make_async_copy(source, target, table_sem.at[n]) for n, (source, target) in enumerate(pieces)]
    for load in loads:
        load.start()
    barrier = pltpu.get_barrier_semaphore()

    def greet(r, carry):
        pl.semaphore_signal(barrier, inc=1, device_id={"len": lax.rem(me + r, LEN)}, device_id_type=MESH)
        return carry

    lax.fori_loop(1, LEN, greet, 0)
    for r in range(1, MEM):
        pl.semaphore_signal(barrier, inc=1, device_id={"mem": lax.rem(plane + r, MEM)}, device_id_type=MESH)
    loads[0].wait()
    sort_phases(0, left_ref, sorted_ref)
    loads[1].wait()
    sort_phases(1, right_ref, sorted_ref)
    pl.semaphore_wait(barrier, LEN + MEM - 2)

    own = []
    for pair in range(2):
        for half in range(2):
            target = in1_ref.at[rows_at(pair * 2048 + me * 64 + half * 32, 32)]
            source = sorted_ref.at[rows_at(classes(me)[2 * pair + half] * 32, 32)]
            own.append(pltpu.make_async_copy(source, target, own_sem.at[2 * pair + half]))
            own[-1].start()
    for pair in range(2):
        for d in partners(me):
            for half in range(2):
                source = sorted_ref.at[rows_at(classes(d)[2 * pair + half] * 32, 32)]
                target = in1_ref.at[rows_at(pair * 2048 + me * 64 + half * 32, 32)]
                send(source, target, sems, pair, {"len": d})
    for pair in range(2):
        fill_levels(pair, me, roughness_ref, waviness_ref, coherence_ref, level_ref)
        fill_twist(pair, me, twist_ref)
    for load in loads[2:]:
        load.wait()
    for copy in own:
        copy.wait()

    own = []
    for pair in range(2):
        settle(in1_ref.at[pl.ds(0, 31 * 64)], sems, pair, other, 1)
        spectra(pair, in1_ref, level_ref, high_ref, low_ref)
        transforms(pair, me, high_ref, low_ref, row_ref, lane_ref, twist_ref, part_ref, out2_ref)
        span = pl.ds(64 * pair, 64)
        target = in2_ref.at[rows_at(me * 128 + 64 * pair, 64)]
        own.append(pltpu.make_async_copy(out2_ref.at[me, span], target, own_sem.at[4 + 2 * pair]))
        quarter = out2_ref.at[pl.ds(8 * plane, 8), span]
        target_mem = members_ref.at[plane, :, span]
        own.append(pltpu.make_async_copy(quarter, target_mem, own_sem.at[5 + 2 * pair]))
        own[-2].start()
        own[-1].start()
        for r in range(1, MEM):
            d = lax.rem(plane + r, MEM)
            send(out2_ref.at[pl.ds(8 * d, 8), span], target_mem, sems, 4 + pair, {"mem": d})
        for start, size, sem in ((0, 64, 2),) if pair == 0 else ((64, 32, 3), (96, 32, 10)):
            for d in partners(me):
                target = in2_ref.at[rows_at(me * 128 + start, size)]
                send(out2_ref.at[d, pl.ds(start, size)], target, sems, sem, {"len": d})
    for copy in own:
        copy.wait()

    settle(members_ref.at[pl.ds(0, 3), :, pl.ds(0, 64)], sems, 4, above, 1)
    gram_half(0, members_ref, total_ref)
    settle(in2_ref.at[pl.ds(0, 31 * 64)], sems, 2, other, 1)
    own = []
    for group in range(4):
        if group % 2 == 0:
            settle(in2_ref.at[pl.ds(0, 31 * 32)], sems, (3, 10)[group // 2], other, 1)
        class_transform(group, in2_ref, class_ref, out3_ref)
        target = in3_ref.at[rows_at(group * 1024 + me * 32, 32)]
        mine = out3_ref.at[rows_at(group * 1024 + me * 32, 32)]
        own.append(pltpu.make_async_copy(mine, target, own_sem.at[8 + group]))
        own[-1].start()
        for d in partners(me):
            send(out3_ref.at[rows_at(group * 1024 + d * 32, 32)], target, sems, 11 + group, {"len": d})
        if group == 1:
            settle(members_ref.at[pl.ds(0, 3), :, pl.ds(0, 64)], sems, 5, above, 1)
            gram_half(1, members_ref, total_ref)
            mine_ref[...] = gram_part(fold_ref, total_ref)
            grams_ref[me] = mine_ref[...]
            for d in partners(me):
                send(mine_ref, grams_ref.at[me], sems, 6, {"len": d})

    settle(grams_ref.at[pl.ds(0, 31)], sems, 6, other, 1)
    summed = lax.fori_loop(0, LEN, lambda n, total: total + grams_ref[n], jnp.zeros((8, LANES), F32))
    planes_ref[MEM] = summed
    planes_ref[plane] = summed
    for r in range(1, MEM):
        send(planes_ref.at[MEM], planes_ref.at[plane], sems, 9, {"mem": lax.rem(plane + r, MEM)})
    for copy in own:
        copy.wait()
    for group in range(4):
        settle(in3_ref.at[pl.ds(0, 31 * 32)], sems, 11 + group, other, 1)
        place(group, in3_ref, profile_ref)
        if group == 0:
            settle(planes_ref.at[pl.ds(0, 3)], sems, 9, above, 1)
            gram = planes_ref[0] + planes_ref[1] + planes_ref[2] + planes_ref[3]
            factor_ref[...] = upper_factor(gram)[:, :32]

    for sem, ref in ((0, in1_ref), (1, in1_ref), (2, in1_ref)):
        settle(ref.at[pl.ds(0, 31 * 64)], sems, sem, other, 0)
    for sem in (3, 10, 11, 12, 13, 14):
        settle(in1_ref.at[pl.ds(0, 31 * 32)], sems, sem, other, 0)
    for pair in range(2):
        settle(members_ref.at[pl.ds(0, 3), :, pl.ds(0, 64)], sems, 4 + pair, above, 0)
    settle(grams_ref.at[pl.ds(0, 31)], sems, 6, other, 0)
    settle(planes_ref.at[pl.ds(0, 3)], sems, 9, above, 0)


def hand_over_kernel(profile_in, factor_in, profile_out, factor_out, sems):
    copies = [
        pltpu.make_async_copy(profile_in, profile_out, sems.at[0]),
        pltpu.make_async_copy(factor_in, factor_out, sems.at[1]),
    ]
    for copy in copies:
        copy.start()
    for copy in copies:
        copy.wait()


def hand_over(profile, factor):
    vmem = pl.BlockSpec(memory_space=pltpu.VMEM)
    hbm = pl.BlockSpec(memory_space=pl.ANY)
    return pl.pallas_call(
        hand_over_kernel,
        out_shape=(jax.ShapeDtypeStruct(profile.shape, F32), jax.ShapeDtypeStruct(factor.shape, F32)),
        in_specs=[vmem, vmem],
        out_specs=(hbm, hbm),
        scratch_shapes=[pltpu.SemaphoreType.DMA((2,))],
        compiler_params=pltpu.CompilerParams(vmem_limit_bytes=8 * 1024 * 1024),
        name="hand_over",
    )(profile, factor)


def pinned(array):
    return pltpu.with_memory_space_constraint(array, pltpu.HBM)


def per_device(phase_left, phase_right, roughness, waviness, coherence):
    row_dft, lane_dft, class_dft, fold = tables()
    smem = pl.BlockSpec(memory_space=pltpu.SMEM)
    vmem = pl.BlockSpec(memory_space=pltpu.VMEM)
    hbm = pl.BlockSpec(memory_space=pltpu.HBM)
    profile, factor = pl.pallas_call(
        road_kernel,
        out_shape=(jax.ShapeDtypeStruct((2, 8, 32768), F32), jax.ShapeDtypeStruct((32, 32), F32)),
        in_specs=[hbm, hbm, smem, smem, smem, hbm, hbm, hbm, hbm],
        out_specs=(vmem, vmem),
        scratch_shapes=[
            pltpu.VMEM((8, 32768), F32),
            pltpu.VMEM((8, 32768), F32),
            pltpu.VMEM(row_dft.shape, BF16),
            pltpu.VMEM(lane_dft.shape, BF16),
            pltpu.VMEM(class_dft.shape, BF16),
            pltpu.VMEM(fold.shape, F32),
            pltpu.VMEM((4096, LANES), F32),
            pltpu.VMEM((4096, LANES), F32),
            pltpu.VMEM((3, 2048, LANES), F32),
            pltpu.VMEM((2, 2048, LANES), F32),
            pltpu.VMEM((4, 2, 256, 256), BF16),
            pltpu.VMEM((4, 2, 256, 256), BF16),
            pltpu.VMEM((2, 2, 256, LANES), F32),
            pltpu.VMEM((LEN, 128, LANES), F32),
            pltpu.VMEM((4096, LANES), F32),
            pltpu.VMEM((MEM, 8, 128, LANES), F32),
            pltpu.VMEM((512, 512), F32),
            pltpu.VMEM((8, LANES), F32),
            pltpu.VMEM((LEN, 8, LANES), F32),
            pltpu.VMEM((MEM + 1, 8, LANES), F32),
            pltpu.VMEM((4096, LANES), F32),
            pltpu.VMEM((4096, LANES), F32),
            pltpu.SemaphoreType.DMA((6,)),
            pltpu.SemaphoreType.DMA((12,)),
            pltpu.SemaphoreType.DMA((2, 15)),
        ],
        compiler_params=pltpu.CompilerParams(
            collective_id=0, has_side_effects=True, vmem_limit_bytes=VMEM_LIMIT
        ),
        name="road_profiles",
    )(
        *(pinned(array) for array in (phase_left, phase_right, roughness, waviness, coherence)),
        *(pinned(jnp.asarray(table)) for table in (row_dft, lane_dft, class_dft, fold)),
    )
    return hand_over(profile, factor)


def solution(mesh):
    placed = (P("mem", "len"), P("mem", "len"), P("mem"), P("mem"), P("mem"))
    return jax.shard_map(
        per_device,
        mesh=mesh,
        in_specs=placed,
        out_specs=(P(None, "mem", "len"), P()),
        check_vma=False,
    )
```

```python
import functools
import math

import jax
import jax.numpy as jnp
import ml_dtypes
import numpy as np
from jax import lax
from jax.experimental import pallas as pl
from jax.experimental.pallas import tpu as pltpu
from jax.sharding import PartitionSpec as P

ANCHOR = 64
POINTS = 1048576
LEN = 32
MEM = 4
ROWS = 128
LANES = 128
F32 = jnp.float32
BF16 = jnp.bfloat16
MESH = pl.DeviceIdType.MESH
PIECES = 4
VMEM_LIMIT = 40 * 1024 * 1024


def halves(table):
    table = np.asarray(table, np.float64)
    high = table.astype(np.float32).astype(ml_dtypes.bfloat16)
    low = (table - high.astype(np.float64)).astype(np.float32).astype(ml_dtypes.bfloat16)
    return np.stack([high, low])


def class_of():
    d = np.arange(LEN)
    rest = np.where(d == 0, 64, 128 - d)
    third = np.where(d == 0, 32, 64 - d)
    fourth = np.where(d == 0, 96, 64 + d)
    return np.stack([d, rest, third, fourth], axis=1)


@functools.lru_cache(None)
def tables():
    turn = 2.0 * math.pi
    w_row = np.arange(ROWS)
    w = w_row // 16 + 8 * (w_row % 16)
    r = np.arange(ROWS)
    row_tables = []
    for a in range(4):
        angle = turn * ((w[:, None] * r[None, :] % 128) / 128.0 + a * r[None, :] / 512.0)
        cos, sin = np.cos(angle), np.sin(angle)
        row_tables.append(halves(np.block([[cos, -sin], [sin, cos]])))
    row_dft = np.stack(row_tables)
    lane = np.arange(LANES)
    e, m = lane // 8, lane % 8
    same = (m[:, None] == m[None, :]).astype(np.float64)
    angle = turn * (e[:, None] * e[None, :] % 16) / 16.0
    cos, sin = 0.5 * same * np.cos(angle), 0.5 * same * np.sin(angle)
    lane_dft = halves(np.block([[cos, sin], [-sin, cos]]))
    v = np.arange(128)
    c = class_of().reshape(LEN, 2, 2).transpose(2, 0, 1).reshape(-1)
    angle = turn * (v[:, None] * c[None, :] % 128) / 128.0
    cos, sin = np.cos(angle), np.sin(angle)
    class_dft = halves(np.block([[cos, -sin], [sin, cos]]))
    index = np.arange(512)
    fold = np.zeros((512, LANES), np.float32)
    for a in range(4):
        fold[index, 32 * a + 8 * (index // 128) + index % 8] = 1.0
    return row_dft, lane_dft, class_dft, fold


@functools.lru_cache(None)
def sine_terms():
    h = np.cos(np.pi * (np.arange(4000) + 0.5) / 4000) * 1.575
    z = h * h
    sin = np.linalg.lstsq(np.stack([h ** (2 * n + 1) for n in range(6)], 1), np.sin(h), rcond=None)[0]
    cos = np.linalg.lstsq(np.stack([z**n for n in range(1, 7)], 1), np.cos(h) - 1.0, rcond=None)[0]
    return [float(x) for x in sin], [float(x) for x in cos]


def cos_sin(phase):
    sin_terms, cos_terms = sine_terms()
    half = phase * 0.5
    z = half * half
    s = jnp.full_like(z, sin_terms[-1])
    for term in sin_terms[-2::-1]:
        s = s * z + term
    s = s * half
    c = jnp.full_like(z, cos_terms[-1])
    for term in cos_terms[-2::-1]:
        c = c * z + term
    c = c * z + 1.0
    return 1.0 - 2.0 * (s * s), 2.0 * (s * c)


def split(x):
    high = x.astype(BF16)
    return high, (x - high.astype(F32)).astype(BF16)


def dot(a, b):
    return jnp.dot(a, b, preferred_element_type=F32)


def order():
    chips = [(2, 2), (1, 2), (2, 1), (3, 2), (2, 3), (0, 2), (2, 0), (1, 1), (3, 3), (1, 3), (3, 1)]
    chips += [(0, 1), (1, 0), (0, 3), (3, 0)]
    return [(dx, dy, dc) for dc in range(2) for dx, dy in chips] + [(0, 0, 1)]


def partners(me):
    x, y, core = lax.div(me, 8), lax.rem(lax.div(me, 2), 4), lax.rem(me, 2)
    for dx, dy, dc in order():
        yield lax.rem(x + dx, 4) * 8 + lax.rem(y + dy, 4) * 2 + lax.rem(core + dc, 2)


def classes(d):
    first = d == 0
    return (d, jnp.where(first, 64, 128 - d), jnp.where(first, 32, 64 - d), jnp.where(first, 96, 64 + d))


def rows_at(start, size):
    return pl.ds(pl.multiple_of(start, 8), size)


def send(source, target, sems, index, device):
    pltpu.make_async_remote_copy(
        source, target, sems.at[0, index], sems.at[1, index], device_id=device, device_id_type=MESH
    ).start()


def settle(ref, sems, index, device, which):
    copy = pltpu.make_async_remote_copy(
        ref, ref, sems.at[0, index], sems.at[1, index], device_id=device, device_id_type=MESH
    )
    if which == 0:
        copy.wait_send()
    else:
        copy.wait_recv()


def unit_turn(numerator, size):
    cos, sin = cos_sin(numerator.astype(F32) * (2.0 * math.pi / size) - math.pi)
    return -cos, -sin


def sort_phases(index, load, ref, sorted_ref):
    for piece in range(PIECES):
        load[piece].wait()
        for i in range(piece * 16 // PIECES, (piece + 1) * 16 // PIECES):
            tiles = [ref[:, i * 2048 + e * 128 : i * 2048 + e * 128 + 128] for e in range(16)]
            sorted_ref[pl.ds(index * 16 + i, 128, stride=32), :] = jnp.concatenate(tiles, axis=0).T


def member_lanes(ref):
    lane = lax.rem(lax.broadcasted_iota(jnp.int32, (8, LANES), 1), 8)
    values = jnp.zeros((8, LANES), F32)
    for m in range(8):
        values = jnp.where(lane == m, ref[m], values)
    return values


def fill_levels(pair, me, roughness_ref, waviness_ref, coherence_ref, level_ref):
    waviness = member_lanes(waviness_ref)
    scale = jnp.sqrt(2.0 * member_lanes(roughness_ref) * (waviness - 1.0) * (1.0 / ANCHOR))
    exponent = -0.5 * waviness
    inverse = 1.0 / member_lanes(coherence_ref)
    row = lax.broadcasted_iota(jnp.int32, (8, LANES), 0)
    lane = lax.broadcasted_iota(jnp.int32, (8, LANES), 1)
    spread = row * 2048 + lax.div(lane, 8) * 128
    for half in range(2):
        offset = spread + classes(me)[2 * pair + half]

        def step(n, carry, half=half, offset=offset):
            freq = (offset + n * 16384).astype(F32)
            amplitude = scale * jnp.exp(exponent * jnp.log(freq * (1.0 / ANCHOR) + 1.0))
            ratio = freq * inverse
            square = ratio * ratio
            coherent = 1.0 / (1.0 + square)
            incoherent = ratio * jnp.sqrt(2.0 + square) * coherent
            rows = rows_at(pair * 1024 + half * 512 + n * 8, 8)
            level_ref[0, rows, :] = amplitude
            level_ref[1, rows, :] = amplitude * coherent
            level_ref[2, rows, :] = amplitude * incoherent
            return carry

        lax.fori_loop(0, 64, step, 0, unroll=4)


def fill_twist(pair, me, twist_ref):
    row = lax.broadcasted_iota(jnp.int32, (8, LANES), 0)
    lane = lax.broadcasted_iota(jnp.int32, (8, LANES), 1)
    for half in range(2):
        place = lax.div(lane, 8) * 128 + classes(me)[2 * pair + half]

        def step(n, carry, half=half, place=place):
            upper = lax.div(n, 16) + 4 * lax.rem(lax.div(n, 2), 8) + 32 * (lax.rem(n, 2) * 8 + row)
            cos, sin = unit_turn(lax.rem(upper * place, POINTS), POINTS)
            rows = rows_at(pair * 1024 + half * 512 + n * 8, 8)
            twist_ref[0, rows, :] = cos
            twist_ref[1, rows, :] = sin
            return carry

        lax.fori_loop(0, 64, step, 0, unroll=4)


def spectra(pair, in_ref, level_ref, high_ref, low_ref):
    def step(index, carry):
        half = lax.div(index, 8)
        low_p = lax.rem(index, 8)
        parts = []
        for q in range(4):
            p = 8 * q + low_p
            start = pair * 2048 + p * 64 + half * 32
            cos_left, sin_left = cos_sin(in_ref[rows_at(start, 16), :])
            cos_right, sin_right = cos_sin(in_ref[rows_at(start + 16, 16), :])
            rows = rows_at(pair * 1024 + half * 512 + p * 16, 16)
            amplitude, first, second = level_ref[0, rows, :], level_ref[1, rows, :], level_ref[2, rows, :]
            parts.append(
                (
                    amplitude * cos_left,
                    amplitude * sin_left,
                    first * cos_left + second * cos_right,
                    first * sin_left + second * sin_right,
                )
            )
        rows = pl.ds(pl.multiple_of(low_p * 16, 16), 16)
        imag_rows = pl.ds(pl.multiple_of(128 + low_p * 16, 16), 16)
        for track in range(2):
            re = [part[2 * track] for part in parts]
            im = [part[2 * track + 1] for part in parts]
            even_re, even_im = re[0] + re[2], im[0] + im[2]
            odd_re, odd_im = re[1] + re[3], im[1] + im[3]
            diff_re, diff_im = re[0] - re[2], im[0] - im[2]
            skew_re, skew_im = re[1] - re[3], im[1] - im[3]
            results = (
                (even_re + odd_re, even_im + odd_im),
                (diff_re - skew_im, diff_im + skew_re),
                (even_re - odd_re, even_im - odd_im),
                (diff_re + skew_im, diff_im - skew_re),
            )
            lanes = slice(track * 128, track * 128 + 128)
            for a, (x, y) in enumerate(results):
                high, low = split(x)
                high_ref[a, half, rows, lanes] = high
                low_ref[a, half, rows, lanes] = low
                high, low = split(y)
                high_ref[a, half, imag_rows, lanes] = high
                low_ref[a, half, imag_rows, lanes] = low
        return carry

    lax.fori_loop(0, 16, step, 0)


def transforms(pair, me, high_ref, low_ref, row_ref, lane_ref, twist_ref, part_ref, out_ref):
    is_first = me == 0
    lane = lax.div(lax.broadcasted_iota(jnp.int32, (1, LANES), 1), 8)
    turns = [unit_turn(lane * classes(me)[2 * pair + half], 2048) for half in range(2)]

    def step(a, carry):
        table_high, table_low = row_ref[a, 0], row_ref[a, 1]
        for half in range(2):
            high, low = high_ref[a, half], low_ref[a, half]
            partial = dot(table_high, high) + dot(table_low, high) + dot(table_high, low)
            rows = pl.ds(pl.multiple_of(pair * 1024 + half * 512 + a * 128, 128), 128)
            cos, sin = twist_ref[0, rows, :], twist_ref[1, rows, :]
            stacked = []
            for track in range(2):
                re = partial[:128, track * 128 : track * 128 + 128]
                im = partial[128:, track * 128 : track * 128 + 128]
                stacked.append(jnp.concatenate([re * cos - im * sin, re * sin + im * cos], axis=1))
            high, low = split(jnp.concatenate(stacked, axis=0))
            done = dot(high, lane_ref[0]) + dot(low, lane_ref[0]) + dot(high, lane_ref[1])
            cos, sin = turns[half]
            re, im = done[:, :128], done[:, 128:]
            part_ref[half, 0] = re * cos - im * sin
            part_ref[half, 1] = re * sin + im * cos
        re0, im0 = part_ref[0, 0, :128, :], part_ref[0, 1, :128, :]
        re1, im1 = part_ref[0, 0, 128:, :], part_ref[0, 1, 128:, :]
        mirror_re0, mirror_im0 = part_ref[1, 0, :128, :], part_ref[1, 1, :128, :]
        mirror_re1, mirror_im1 = part_ref[1, 0, 128:, :], part_ref[1, 1, 128:, :]
        sum_re0, sum_re1 = re0 + mirror_re0, re1 + mirror_re1
        gap_im0, gap_im1 = im0 - mirror_im0, im1 - mirror_im1
        packed = [
            [sum_re0 - gap_im1, gap_im0 + sum_re1],
            [sum_re0 + gap_im1, sum_re1 - gap_im0],
        ]
        if pair == 0:
            alone = [[re0 + re0, re1 + re1], [mirror_re0 + mirror_re0, mirror_re1 + mirror_re1]]
            packed = [[jnp.where(is_first, alone[n][x], packed[n][x]) for x in range(2)] for n in range(2)]
        for n in range(2):
            for x in range(2):
                for wl in range(8):
                    for g in range(2):
                        start = pair * 64 + g * 32 + n * 16 + x * 8
                        out_ref[4 * wl + a, start : start + 8, :] = packed[n][x][
                            wl * 16 + g * 8 : wl * 16 + g * 8 + 8, :
                        ]
        return carry

    lax.fori_loop(0, 4, step, 0)


def gram_half(pair, members_ref, total_ref):
    product = functools.partial(
        lax.dot_general, dimension_numbers=(((0,), (0,)), ((), ())), preferred_element_type=F32
    )

    def step(n):
        span = pl.ds(64 * pair, 64)
        rows = [members_ref[z, pl.ds(4 * n, 4), span].reshape(256, LANES) for z in range(MEM)]
        high, low = split(jnp.concatenate(rows, axis=1))
        part = product(high, high) + product(low, high) + product(high, low)
        total_ref[...] = part if pair == 0 and n == 0 else total_ref[...] + part

    step(0)
    step(1)


def gram_part(fold_ref, total_ref):
    row = lax.broadcasted_iota(jnp.int32, (512, 512), 0)
    column = lax.broadcasted_iota(jnp.int32, (512, 512), 1)
    same = lax.rem(lax.div(row, 8), 16) == lax.rem(lax.div(column, 8), 16)
    kept = jnp.where(same, total_ref[...], 0.0)
    right = jnp.dot(kept, fold_ref[...], preferred_element_type=F32, precision=lax.Precision.HIGHEST)
    row = lax.broadcasted_iota(jnp.int32, (512, LANES), 0)
    lane = lax.broadcasted_iota(jnp.int32, (512, LANES), 1)
    right = jnp.where(lax.div(row, 128) == lax.div(lane, 32), right, 0.0)
    return jnp.sum(right.reshape(64, 8, LANES), axis=0) * (128.0 / (2.0 * POINTS))


def upper_factor(gram):
    row = lax.broadcasted_iota(jnp.int32, (32, LANES), 0)
    lane = lax.broadcasted_iota(jnp.int32, (32, LANES), 1)
    tall = jnp.concatenate([gram] * 4, axis=0)
    tall = jnp.where(lax.div(row, 8) == lax.div(lane, 32), tall, 0.0)
    pick_row = lax.broadcasted_iota(jnp.int32, (LANES, LANES), 0)
    pick_lane = lax.broadcasted_iota(jnp.int32, (LANES, LANES), 1)
    pick = jnp.where(lax.rem(pick_row, 32) == pick_lane, 1.0, 0.0)
    matrix = jnp.dot(tall, pick, preferred_element_type=F32, precision=lax.Precision.HIGHEST)

    def step(n, carry):
        rest, upper = carry
        column = jnp.sum(jnp.where(lane == n, rest, 0.0), axis=1, keepdims=True)
        line = jnp.sum(jnp.where(row == n, rest, 0.0), axis=0, keepdims=True)
        pivot = jnp.sum(jnp.where(row[:, 0:1] == n, column, 0.0), axis=0, keepdims=True)
        inverse = 1.0 / jnp.sqrt(pivot)
        line = jnp.where(lane[0:1] >= n, line * inverse, 0.0)
        column = column * inverse
        return rest - column * line, jnp.where(row == n, line, upper)

    return lax.fori_loop(0, 32, step, (matrix, jnp.zeros_like(matrix)))[1]


def class_transform(group, in_ref, table_ref, out_ref):
    for n in range(2):
        columns = []
        for index in range(2):
            u2 = 4 * group + 2 * n + index
            start = (u2 // 8) * 32 + u2 % 8
            parts = [in_ref[pl.ds(start + 8 * x + 16 * half, 64, stride=64), :] for x in range(2) for half in range(2)]
            columns.append(jnp.concatenate(parts, axis=0))
        high, low = split(jnp.concatenate(columns, axis=1))
        done = dot(table_ref[0], high) + dot(table_ref[1], high) + dot(table_ref[0], low)
        for index in range(2):
            for track in range(2):
                out_ref[pl.ds(group * 1024 + 4 * track + 2 * n + index, 128, stride=8), :] = done[
                    track * 128 : track * 128 + 128, index * 128 : index * 128 + 128
                ]


def place(group, in_ref, out_ref):
    def step(index, carry):
        vl = lax.div(index, 2)
        track = lax.rem(index, 2)
        base = group * 1024 + vl * 8 + track * 4
        rows = [in_ref[pl.ds(base + low, 32, stride=32), :] for low in range(4)]
        turned = jnp.concatenate(rows, axis=0).T
        for u3 in range(16):
            column = pl.multiple_of((vl * 64 + u3 * 4 + group) * 128, 128)
            out_ref[track, :, pl.ds(column, 128)] = turned[8 * u3 : 8 * u3 + 8, :]
        return carry

    lax.fori_loop(0, 8, step, 0, unroll=2)


def road_kernel(
    left_hbm, right_hbm, roughness_ref, waviness_ref, coherence_ref, row_hbm, lane_hbm, class_hbm, fold_hbm,
    profile_ref, factor_ref,
    left_ref, right_ref, row_ref, lane_ref, class_ref, fold_ref, sorted_ref, in1_ref, level_ref, twist_ref, high_ref, low_ref, part_ref,
    out2_ref, in2_ref, members_ref, total_ref, mine_ref, grams_ref, planes_ref, out3_ref, in3_ref,
    table_sem, own_sem, sems,
):
    me = lax.axis_index("len")
    plane = lax.axis_index("mem")
    other = {"len": lax.rem(me + 1, LEN)}
    above = {"mem": lax.rem(plane + 1, MEM)}
    pieces = []
    for source, target in ((left_hbm, left_ref), (right_hbm, right_ref)):
        for n in range(PIECES):
            span = pl.ds(n * (32768 // PIECES), 32768 // PIECES)
            pieces.append((source.at[:, span], target.at[:, span]))
    pieces += [(row_hbm, row_ref), (lane_hbm, lane_ref), (class_hbm, class_ref), (fold_hbm, fold_ref)]
    loads = [pltpu.make_async_copy(source, target, table_sem.at[n]) for n, (source, target) in enumerate(pieces)]
    for load in loads:
        load.start()
    barrier = pltpu.get_barrier_semaphore()

    def greet(r, carry):
        pl.semaphore_signal(barrier, inc=1, device_id={"len": lax.rem(me + r, LEN)}, device_id_type=MESH)
        return carry

    lax.fori_loop(1, LEN, greet, 0)
    for r in range(1, MEM):
        pl.semaphore_signal(barrier, inc=1, device_id={"mem": lax.rem(plane + r, MEM)}, device_id_type=MESH)
    sort_phases(0, loads[:PIECES], left_ref, sorted_ref)
    sort_phases(1, loads[PIECES:], right_ref, sorted_ref)
    pl.semaphore_wait(barrier, LEN + MEM - 2)

    own = []
    for pair in range(2):
        for half in range(2):
            target = in1_ref.at[rows_at(pair * 2048 + me * 64 + half * 32, 32)]
            source = sorted_ref.at[rows_at(classes(me)[2 * pair + half] * 32, 32)]
            own.append(pltpu.make_async_copy(source, target, own_sem.at[2 * pair + half]))
            own[-1].start()
    for pair in range(2):
        for d in partners(me):
            for half in range(2):
                source = sorted_ref.at[rows_at(classes(d)[2 * pair + half] * 32, 32)]
                target = in1_ref.at[rows_at(pair * 2048 + me * 64 + half * 32, 32)]
                send(source, target, sems, pair, {"len": d})
    for pair in range(2):
        fill_levels(pair, me, roughness_ref, waviness_ref, coherence_ref, level_ref)
        fill_twist(pair, me, twist_ref)
    for load in loads[2 * PIECES :]:
        load.wait()
    for copy in own:
        copy.wait()

    own = []
    for pair in range(2):
        settle(in1_ref.at[pl.ds(0, 31 * 64)], sems, pair, other, 1)
        spectra(pair, in1_ref, level_ref, high_ref, low_ref)
        transforms(pair, me, high_ref, low_ref, row_ref, lane_ref, twist_ref, part_ref, out2_ref)
        span = pl.ds(64 * pair, 64)
        target = in2_ref.at[rows_at(me * 128 + 64 * pair, 64)]
        own.append(pltpu.make_async_copy(out2_ref.at[me, span], target, own_sem.at[4 + 2 * pair]))
        quarter = out2_ref.at[pl.ds(8 * plane, 8), span]
        target_mem = members_ref.at[plane, :, span]
        own.append(pltpu.make_async_copy(quarter, target_mem, own_sem.at[5 + 2 * pair]))
        own[-2].start()
        own[-1].start()
        for r in range(1, MEM):
            d = lax.rem(plane + r, MEM)
            send(out2_ref.at[pl.ds(8 * d, 8), span], target_mem, sems, 4 + pair, {"mem": d})
        for start, size, sem in ((0, 64, 2),) if pair == 0 else ((64, 32, 3), (96, 32, 10)):
            for d in partners(me):
                target = in2_ref.at[rows_at(me * 128 + start, size)]
                send(out2_ref.at[d, pl.ds(start, size)], target, sems, sem, {"len": d})
    for copy in own:
        copy.wait()

    settle(members_ref.at[pl.ds(0, 3), :, pl.ds(0, 64)], sems, 4, above, 1)
    gram_half(0, members_ref, total_ref)
    settle(in2_ref.at[pl.ds(0, 31 * 64)], sems, 2, other, 1)
    own = []
    for group in range(4):
        if group % 2 == 0:
            settle(in2_ref.at[pl.ds(0, 31 * 32)], sems, (3, 10)[group // 2], other, 1)
        class_transform(group, in2_ref, class_ref, out3_ref)
        target = in3_ref.at[rows_at(group * 1024 + me * 32, 32)]
        mine = out3_ref.at[rows_at(group * 1024 + me * 32, 32)]
        own.append(pltpu.make_async_copy(mine, target, own_sem.at[8 + group]))
        own[-1].start()
        for d in partners(me):
            send(out3_ref.at[rows_at(group * 1024 + d * 32, 32)], target, sems, 11 + group, {"len": d})
        if group == 1:
            settle(members_ref.at[pl.ds(0, 3), :, pl.ds(0, 64)], sems, 5, above, 1)
            gram_half(1, members_ref, total_ref)
            mine_ref[...] = gram_part(fold_ref, total_ref)
            grams_ref[me] = mine_ref[...]
            for d in partners(me):
                send(mine_ref, grams_ref.at[me], sems, 6, {"len": d})

    settle(grams_ref.at[pl.ds(0, 31)], sems, 6, other, 1)
    summed = lax.fori_loop(0, LEN, lambda n, total: total + grams_ref[n], jnp.zeros((8, LANES), F32))
    planes_ref[MEM] = summed
    planes_ref[plane] = summed
    for r in range(1, MEM):
        send(planes_ref.at[MEM], planes_ref.at[plane], sems, 9, {"mem": lax.rem(plane + r, MEM)})
    for copy in own:
        copy.wait()
    for group in range(4):
        settle(in3_ref.at[pl.ds(0, 31 * 32)], sems, 11 + group, other, 1)
        place(group, in3_ref, profile_ref)
        if group == 0:
            settle(planes_ref.at[pl.ds(0, 3)], sems, 9, above, 1)
            gram = planes_ref[0] + planes_ref[1] + planes_ref[2] + planes_ref[3]
            factor_ref[...] = upper_factor(gram)[:, :32]

    for sem, ref in ((0, in1_ref), (1, in1_ref), (2, in1_ref)):
        settle(ref.at[pl.ds(0, 31 * 64)], sems, sem, other, 0)
    for sem in (3, 10, 11, 12, 13, 14):
        settle(in1_ref.at[pl.ds(0, 31 * 32)], sems, sem, other, 0)
    for pair in range(2):
        settle(members_ref.at[pl.ds(0, 3), :, pl.ds(0, 64)], sems, 4 + pair, above, 0)
    settle(grams_ref.at[pl.ds(0, 31)], sems, 6, other, 0)
    settle(planes_ref.at[pl.ds(0, 3)], sems, 9, above, 0)


def hand_over_kernel(profile_in, factor_in, profile_out, factor_out, sems):
    copies = [
        pltpu.make_async_copy(profile_in, profile_out, sems.at[0]),
        pltpu.make_async_copy(factor_in, factor_out, sems.at[1]),
    ]
    for copy in copies:
        copy.start()
    for copy in copies:
        copy.wait()


def hand_over(profile, factor):
    vmem = pl.BlockSpec(memory_space=pltpu.VMEM)
    hbm = pl.BlockSpec(memory_space=pl.ANY)
    return pl.pallas_call(
        hand_over_kernel,
        out_shape=(jax.ShapeDtypeStruct(profile.shape, F32), jax.ShapeDtypeStruct(factor.shape, F32)),
        in_specs=[vmem, vmem],
        out_specs=(hbm, hbm),
        scratch_shapes=[pltpu.SemaphoreType.DMA((2,))],
        compiler_params=pltpu.CompilerParams(vmem_limit_bytes=8 * 1024 * 1024),
        name="hand_over",
    )(profile, factor)


def pinned(array):
    return pltpu.with_memory_space_constraint(array, pltpu.HBM)


def per_device(phase_left, phase_right, roughness, waviness, coherence):
    row_dft, lane_dft, class_dft, fold = tables()
    smem = pl.BlockSpec(memory_space=pltpu.SMEM)
    vmem = pl.BlockSpec(memory_space=pltpu.VMEM)
    hbm = pl.BlockSpec(memory_space=pltpu.HBM)
    profile, factor = pl.pallas_call(
        road_kernel,
        out_shape=(jax.ShapeDtypeStruct((2, 8, 32768), F32), jax.ShapeDtypeStruct((32, 32), F32)),
        in_specs=[hbm, hbm, smem, smem, smem, hbm, hbm, hbm, hbm],
        out_specs=(vmem, vmem),
        scratch_shapes=[
            pltpu.VMEM((8, 32768), F32),
            pltpu.VMEM((8, 32768), F32),
            pltpu.VMEM(row_dft.shape, BF16),
            pltpu.VMEM(lane_dft.shape, BF16),
            pltpu.VMEM(class_dft.shape, BF16),
            pltpu.VMEM(fold.shape, F32),
            pltpu.VMEM((4096, LANES), F32),
            pltpu.VMEM((4096, LANES), F32),
            pltpu.VMEM((3, 2048, LANES), F32),
            pltpu.VMEM((2, 2048, LANES), F32),
            pltpu.VMEM((4, 2, 256, 256), BF16),
            pltpu.VMEM((4, 2, 256, 256), BF16),
            pltpu.VMEM((2, 2, 256, LANES), F32),
            pltpu.VMEM((LEN, 128, LANES), F32),
            pltpu.VMEM((4096, LANES), F32),
            pltpu.VMEM((MEM, 8, 128, LANES), F32),
            pltpu.VMEM((512, 512), F32),
            pltpu.VMEM((8, LANES), F32),
            pltpu.VMEM((LEN, 8, LANES), F32),
            pltpu.VMEM((MEM + 1, 8, LANES), F32),
            pltpu.VMEM((4096, LANES), F32),
            pltpu.VMEM((4096, LANES), F32),
            pltpu.SemaphoreType.DMA((2 * PIECES + 4,)),
            pltpu.SemaphoreType.DMA((12,)),
            pltpu.SemaphoreType.DMA((2, 15)),
        ],
        compiler_params=pltpu.CompilerParams(
            collective_id=0, has_side_effects=True, vmem_limit_bytes=VMEM_LIMIT
        ),
        name="road_profiles",
    )(
        *(pinned(array) for array in (phase_left, phase_right, roughness, waviness, coherence)),
        *(pinned(jnp.asarray(table)) for table in (row_dft, lane_dft, class_dft, fold)),
    )
    return hand_over(profile, factor)


def solution(mesh):
    placed = (P("mem", "len"), P("mem", "len"), P("mem"), P("mem"), P("mem"))
    return jax.shard_map(
        per_device,
        mesh=mesh,
        in_specs=placed,
        out_specs=(P(None, "mem", "len"), P()),
        check_vma=False,
    )
```
